32 devices in a mesh: parts: 2 (over x), row: 8 (over z, core), col: 2 (over y).
Axes of the slice: x: 2, y: 2, z: 4, core: 2. Of those that a mesh axis runs over, the one named last changes fastest.
Arguments:
- pair_features_map: bfloat16 [64, 1024, 512], P(None, ('parts', 'row'), 'col'), parts along dimension 1, may hold values from -6 to 6
- labels: int32 [1024, 512], P(('parts', 'row', 'col')), parts along dimension 0, may hold values from 0 to 36, as said below
- lengths: int32 [2], P('parts'), parts along dimension 0, may hold values from 256 to 512
- conv_weight: bfloat16 [3, 3, 64, 64], replicated, may hold values from -0.25 to 0.25
- conv_bias: float32 [64], replicated, may hold values from -3 to 3
- head_weight: bfloat16 [37, 64], replicated, may hold values from -2.390625 to 2.390625
- head_bias: float32 [37], replicated, may hold values from -4 to 4
Outputs:
- pair_gradient: bfloat16 [64, 1024, 512], P(None, ('parts', 'row'), 'col'), parts along dimension 1
- grad_conv_weight: float32 [6, 3, 64, 64], P('parts'), parts along dimension 0
- grad_conv_bias: float32 [128], P('parts'), parts along dimension 0
- grad_head_weight: float32 [74, 64], P('parts'), parts along dimension 0
- grad_head_bias: float32 [74], P('parts'), parts along dimension 0
- loss: float32 [2], P('parts'), parts along dimension 0
The draws below stay inside these ranges and needn't reach their ends.
There are 2 independent parts, one for each index of `parts`. The reference program is written for one: setup_inputs(seed, part) draws one part's arguments, and reference() takes and returns one part's arrays. A program takes and returns all parts, laid end to end along the dimension named above; an argument that names none is the same for every part. Nothing has to cross between parts.
Inputs may be any that keep to these rules, and one draw needn't show every extreme that they name: labels[i, j] equals labels[j, i] for every pair.
All inputs are finite; a program needn't handle non-finite values.
Results may differ from the reference program's by a relative error of at most 0.0067.
Values may be sent and summed in bfloat16 or wider, within the bound.
No kernel may reach another device: no remote copies, remote signals or barrier semaphores. Data moves between devices by JAX's collectives and lax.ppermute only.
A program may use at most 128 MiB of HBM per device.

```python
import jax
import jax.numpy as jnp
from jax import lax

CH = 64
NBIN = 37
DILATION_STEP = 4
RESIDUE_COUNT = 512


def draw_labels(key, part):
    values = jax.random.randint(key, (RESIDUE_COUNT, RESIDUE_COUNT), 0, NBIN, dtype=jnp.int32)
    row_index = lax.broadcasted_iota(jnp.int32, (RESIDUE_COUNT, RESIDUE_COUNT), 0)
    col_index = lax.broadcasted_iota(jnp.int32, (RESIDUE_COUNT, RESIDUE_COUNT), 1)
    return jnp.where(row_index <= col_index, values, values.T)


def level_of(stream_key, shape, shards, least, largest):
    def one(axis_at, parts):
        heights = jax.random.uniform(jax.random.fold_in(jax.random.fold_in(stream_key, 6), axis_at), (parts,), jnp.float32, least / len(shards), largest / len(shards))
        return jnp.repeat(jnp.exp(heights), shape[axis_at] // parts).reshape((-1,) + (1,) * (len(shape) - axis_at - 1))

    factor_of = one(*shards[0])
    for cut in shards[1:]:
        factor_of = factor_of * one(*cut)
    return factor_of


def normal_values(own_key, shape, width, limit, shards=(), kind=jnp.bfloat16):
    drawn = jax.random.normal(own_key, shape, jnp.float32) * width
    if len(shards) > 0:
        drawn = level_of(own_key, shape, shards, -0.22, 0.18) * drawn
    return jnp.clip(drawn, min=-limit, max=limit).astype(kind)


def setup_inputs(seed: int = 0, part: int = 0) -> dict:
    arg_keys = jax.random.split(jax.random.key(seed), 8)
    part_splits = jax.random.split(jax.random.fold_in(arg_keys[7], part), 8)
    return {
        "pair_features_map": normal_values(part_splits[0], (CH, RESIDUE_COUNT, RESIDUE_COUNT), 1.0, 6.0, ((1, 8), (2, 2))),
        "labels": draw_labels(jax.random.fold_in(jax.random.fold_in(arg_keys[7], part), 71), part),
        "lengths": jax.random.randint(part_splits[2], (1,), RESIDUE_COUNT // 2, RESIDUE_COUNT + 1).astype(jnp.int32),
        "conv_weight": normal_values(arg_keys[3], (3, 3, CH, CH), (9 * CH) ** -0.5, 0.25),
        "conv_bias": normal_values(arg_keys[4], (CH,), 0.5, 3.0, (), jnp.float32),
        "head_weight": normal_values(arg_keys[5], (NBIN, CH), 0.4, 2.390625),
        "head_bias": normal_values(arg_keys[6], (NBIN,), 1.0, 4.0, (), jnp.float32),
    }


def elu_value(field):
    return jnp.where(field > 0, field, jnp.expm1(jnp.minimum(field, 0.0)))


def reference(pair_features_map, labels, lengths, conv_weight, conv_bias, head_weight, head_bias):
    top_accuracy = lax.Precision.HIGHEST
    numeric_module = ("NCHW", "OIHW", "NCHW")
    input_arrays = pair_features_map.astype(jnp.float32)
    filter_weight = conv_weight.astype(jnp.float32)
    before_activation = lax.conv_general_dilated(input_arrays[None], filter_weight.transpose(2, 3, 0, 1), (1, 1), ((DILATION_STEP, DILATION_STEP), (DILATION_STEP, DILATION_STEP)), rhs_dilation=(DILATION_STEP, DILATION_STEP), dimension_numbers=numeric_module, precision=top_accuracy)[0]
    before_activation = before_activation + conv_bias[:, None, None]
    hidden = elu_value(before_activation).astype(jnp.bfloat16)
    hidden32 = hidden.astype(jnp.float32)
    head32 = head_weight.astype(jnp.float32)
    direct = jnp.einsum("kc,cij->kij", head32, hidden32, precision=top_accuracy)
    logits = 0.5 * (direct + direct.transpose(0, 2, 1)) + head_bias[:, None, None]
    row_ids = lax.broadcasted_iota(jnp.int32, (RESIDUE_COUNT, RESIDUE_COUNT), 0)
    col_ids = lax.broadcasted_iota(jnp.int32, (RESIDUE_COUNT, RESIDUE_COUNT), 1)
    extent = lengths[0]
    valid = ((row_ids < extent) & (col_ids < extent)).astype(jnp.float32)
    count = (extent * extent).astype(jnp.float32)
    onehot = (lax.broadcasted_iota(jnp.int32, (NBIN, 1, 1), 0) == labels[None]).astype(jnp.float32)
    lse = jnp.log(jnp.sum(jnp.exp(logits), axis=0))
    picked = jnp.sum(onehot * logits, axis=0)
    loss = jnp.sum(valid * (lse - picked)) / count
    dlogits = (valid[None] * (jnp.exp(logits - lse[None]) - onehot) / count).astype(jnp.bfloat16)
    dlog32 = dlogits.astype(jnp.float32)
    grad_head_weight = 0.5 * (jnp.einsum("kij,cij->kc", dlog32, hidden32, precision=top_accuracy) + jnp.einsum("kij,cji->kc", dlog32, hidden32, precision=top_accuracy))
    grad_head_bias = jnp.sum(dlog32, axis=(1, 2))
    back = jnp.einsum("kc,kij->cij", head32, dlog32, precision=top_accuracy)
    dhidden = 0.5 * (back + back.transpose(0, 2, 1))
    slope = jnp.where(before_activation > 0, 1.0, jnp.exp(jnp.minimum(before_activation, 0.0)))
    preact_gradient = (dhidden * slope).astype(jnp.bfloat16)
    preact_gradient_f32 = preact_gradient.astype(jnp.float32)
    bordered_input = jnp.pad(input_arrays, ((0, 0), (DILATION_STEP, DILATION_STEP), (DILATION_STEP, DILATION_STEP)))
    rows_out = []
    for offset_row in range(3):
        cols_out = []
        for offset_column in range(3):
            sliding_patch = bordered_input[:, offset_row * DILATION_STEP:offset_row * DILATION_STEP + RESIDUE_COUNT, offset_column * DILATION_STEP:offset_column * DILATION_STEP + RESIDUE_COUNT]
            cols_out.append(jnp.einsum("oij,cij->oc", preact_gradient_f32, sliding_patch, precision=top_accuracy))
        rows_out.append(jnp.stack(cols_out))
    grad_conv_weight = jnp.stack(rows_out)
    grad_conv_bias = jnp.sum(preact_gradient_f32, axis=(1, 2))
    reversed_kernel = filter_weight[::-1, ::-1].transpose(3, 2, 0, 1)
    pair_gradient = lax.conv_general_dilated(preact_gradient_f32[None], reversed_kernel, (1, 1), ((DILATION_STEP, DILATION_STEP), (DILATION_STEP, DILATION_STEP)), rhs_dilation=(DILATION_STEP, DILATION_STEP), dimension_numbers=numeric_module, precision=top_accuracy)[0]
    return (pair_gradient.astype(jnp.bfloat16), grad_conv_weight, grad_conv_bias, grad_head_weight, grad_head_bias, loss.reshape(1))
```

```python
import functools

import jax
import jax.numpy as jnp
from jax import lax
from jax.experimental import pallas as pl
from jax.experimental.pallas import tpu as pltpu
from jax.sharding import PartitionSpec as P

DIL = 4
ROWS = ("row", "col")
F32 = jnp.float32
BF16 = jnp.bfloat16


def col_exchange(to_left, to_right):
    count = lax.axis_size("col")
    if count == 2:
        at_zero = lax.axis_index("col") == 0
        got = lax.ppermute(jnp.where(at_zero, to_right, to_left), "col", [(0, 1), (1, 0)])
        none = jnp.zeros_like(got)
        return jnp.where(at_zero, none, got), jnp.where(at_zero, got, none)
    from_left = lax.ppermute(to_right, "col", [(i, i + 1) for i in range(count - 1)])
    from_right = lax.ppermute(to_left, "col", [(i + 1, i) for i in range(count - 1)])
    return from_left, from_right


def row_exchange(head, tail):
    count = lax.axis_size("row")
    above = lax.ppermute(tail, "row", [(i, i + 1) for i in range(count - 1)])
    below = lax.ppermute(head, "row", [(i + 1, i) for i in range(count - 1)])
    return above, below


def side_lanes(left, right):
    gap = jnp.zeros(left.shape[:-1] + (128 - 2 * DIL,), left.dtype)
    return jnp.concatenate([left, gap, right], axis=-1)


def take(ref, start, count, stride, tiles):
    step = ref.shape[0] // tiles
    return jnp.concatenate(
        [ref[pl.ds(start + step * u, count, stride=stride), :] for u in range(tiles)], axis=1
    )


def put(ref, start, stride, value):
    tiles = value.shape[1] // 128
    step = ref.shape[0] // tiles
    for u in range(tiles):
        ref[pl.ds(start + step * u, value.shape[0], stride=stride), :] = value[
            :, 128 * u : 128 * (u + 1)
        ]


def shifted(row, side):
    width = row.shape[1]
    lane = lax.broadcasted_iota(jnp.int32, side.shape, 1)
    before = pltpu.roll(row, DIL, 1)
    after = pltpu.roll(row, width - DIL, 1)
    first = jnp.where(lane < DIL, side, before[:, :128])
    last = jnp.where(lane >= 128 - DIL, side, after[:, width - 128 :])
    if width > 128:
        first = jnp.concatenate([first, before[:, 128:]], axis=1)
        last = jnp.concatenate([after[:, : width - 128], last], axis=1)
    return jnp.concatenate([first.astype(BF16), row.astype(BF16), last.astype(BF16)], axis=0)


def forward_kernel(scal, x, top, bot, side, w, bias, hw, xs, hid, slope, direct, *rest, rows, q):
    sends = rest[:q]
    main, sides, bordered, turned = rest[q:]
    step = pl.program_id(0)
    channels = w.shape[0]
    high = rows + 2 * DIL
    nb = hw.shape[0]
    tiles = x.shape[2] // 128

    @pl.when(step == 0)
    def _():
        def fill(c, _):
            base = pl.multiple_of(c * high, 8)
            body = x[c].astype(F32)
            rim = jnp.concatenate([top[c].astype(F32), bot[c].astype(F32)], axis=0)
            for u in range(tiles):
                at = base + u * channels * high
                lanes = slice(128 * u, 128 * (u + 1))
                main[pl.ds(at, rows), :] = body[:, lanes]
                main[pl.ds(at + rows, 2 * DIL), :] = rim[:, lanes]
            sides[pl.ds(base, high), :] = side[c].astype(F32)
            return 0

        lax.fori_loop(0, channels, fill, 0, unroll=4)

    for ii in range(8):
        i = step * 8 + ii
        at = jnp.where(i < DIL, i + rows, jnp.where(i < rows + DIL, i - DIL, i))
        row = take(main, at, channels, high, tiles)
        edge = sides[pl.ds(i, channels, stride=high), :]
        three = shifted(row, edge)
        bordered[i] = three
        xs[ii] = three

    @pl.when(step > 0)
    def _():
        for ii in range(8):
            i = (step - 1) * 8 + ii
            window = jnp.concatenate([bordered[i + DIL * a] for a in range(3)], axis=0)
            pre = jnp.dot(w[...], window, preferred_element_type=F32) + bias[...]
            grown = jnp.exp(jnp.minimum(pre, 0.0))
            h = jnp.where(pre > 0, pre, grown - 1.0).astype(BF16)
            hid[ii] = h
            slope[ii] = jnp.where(pre > 0, 1.0, grown).astype(BF16)
            put(direct, i, rows, jnp.dot(hw[...], h, preferred_element_type=F32))

    @pl.when(step == pl.num_programs(0) - 1)
    def _():
        for m in range(sends[0].shape[0]):
            for u in range(tiles):
                at = nb * rows * u + 2 * rows * m
                pair = direct[at : at + 2 * rows, :].T.astype(BF16)
                turned[2 * u, m] = pair[:rows]
                turned[2 * u + 1, m] = pair[rows:]
        for t in range(q):
            sends[t][...] = turned[scal[0] ^ t]


def middle_kernel(scal, hb, *rest, q, nbins):
    direct, labels, hid, slope, hwt = rest[:5]
    got = rest[5 : 5 + q]
    dpre, small, dl, hacc, bacc, cacc, lacc = rest[5 + q :]
    step = pl.program_id(0)
    tiles, nb = direct.shape[:2]
    channels = hwt.shape[0]

    @pl.when(step == 0)
    def _():
        hacc[...] = jnp.zeros_like(hacc)
        bacc[...] = jnp.zeros_like(bacc)
        cacc[...] = jnp.zeros_like(cacc)
        lacc[...] = jnp.zeros_like(lacc)
        dl[...] = jnp.zeros_like(dl)

    extent = scal[3]
    lane = lax.broadcasted_iota(jnp.int32, (8, 128), 1)
    row_ids = scal[1] + step * 8 + lax.broadcasted_iota(jnp.int32, (8, 128), 0)
    low = lane < 64
    area = (extent * extent).astype(F32)
    for u in range(tiles):
        lanes = slice(128 * u, 128 * (u + 1))
        col_ids = scal[2] + 128 * u + lane
        valid = jnp.where((row_ids < extent) & (col_ids < extent), 1.0, 0.0)
        wanted = labels[:, lanes]
        logits = []
        for m in range((nbins + 1) // 2):
            parts = [got[t][m].astype(F32) for t in range(q)]
            bit = 1
            while bit < q:
                swap = (scal[0] & bit) != 0
                parts = [jnp.where(swap, parts[s ^ bit], parts[s]) for s in range(q)]
                bit *= 2
            one, two = parts[2 * u], parts[2 * u + 1]
            mirror = (
                jnp.where(low, one, pltpu.roll(two, 64, 1)),
                jnp.where(low, pltpu.roll(one, 64, 1), two),
            )
            for k in range(2 * m, min(2 * m + 2, nbins)):
                logits.append(0.5 * (direct[u, k] + mirror[k - 2 * m]) + hb[k])
        peak = functools.reduce(jnp.maximum, logits)
        picked = functools.reduce(
            lambda a, b: a + b,
            [jnp.where(wanted == k, logits[k], 0.0) for k in range(nbins)],
        )
        powers = [jnp.exp(v - peak) for v in logits]
        total = functools.reduce(lambda a, b: a + b, powers)
        lacc[...] += valid * (peak + jnp.log(total) - picked)
        inverse = 1.0 / total
        scale = valid / area
        for k in range(nbins):
            d = (powers[k] * inverse - jnp.where(wanted == k, 1.0, 0.0)) * scale
            d = d.astype(BF16).astype(F32)
            at = 8 * (nb * u + k)
            dl[at : at + 8, :] = d
            bacc[8 * k : 8 * k + 8, :] += d

    for ii in range(8):
        d = take(dl, ii, nb, 8, tiles).astype(BF16)
        back = jnp.dot(hwt[...], d, preferred_element_type=F32)
        p = (back * slope[ii].astype(F32)).astype(BF16)
        dpre[ii] = p
        cacc[...] += p.astype(F32)
        hacc[0:nb, 0:channels] += lax.dot_general(
            d, hid[ii], (((1,), (1,)), ((), ())), preferred_element_type=F32
        )

    @pl.when(step == pl.num_programs(0) - 1)
    def _():
        spot = lax.broadcasted_iota(jnp.int32, small.shape, 1)
        sums = jnp.sum(bacc[...].reshape(nb, 8, 128), axis=1)
        sums = jnp.sum(sums, axis=1, keepdims=True)
        sums = jnp.concatenate([sums, jnp.zeros((channels - nb, 1), F32)], axis=0)
        biases = jnp.sum(cacc[...], axis=1, keepdims=True)
        loss = jnp.sum(jnp.sum(lacc[...], axis=1, keepdims=True), axis=0, keepdims=True)
        small[...] = jnp.where(
            spot < channels,
            hacc[...],
            jnp.where(spot == channels, sums, jnp.where(spot == channels + 1, biases, loss)),
        )


def weight_kernel(xs, dpre, small, out, acc, padded, *, rows):
    step = pl.program_id(0)
    channels = dpre.shape[1]
    wide = 3 * channels

    @pl.when(step == 0)
    def _():
        acc[...] = jnp.zeros_like(acc)
        padded[0:8] = jnp.zeros((8,) + padded.shape[1:], BF16)
        padded[8 : 8 + rows] = dpre[...]
        padded[8 + rows : 16 + rows] = jnp.zeros((8,) + padded.shape[1:], BF16)

    left = []
    for ii in range(8):
        i = step * 8 + ii + 8
        left.append(jnp.concatenate([padded[i - DIL * a] for a in range(3)], axis=0))
    left = jnp.concatenate(left, axis=1)
    right = jnp.concatenate([xs[ii] for ii in range(8)], axis=1)
    acc[...] += lax.dot_general(
        left, right, (((1,), (1,)), ((), ())), preferred_element_type=F32
    )

    @pl.when(step == pl.num_programs(0) - 1)
    def _():
        half = wide // 2
        out[0:wide, :] = acc[:, 0:128]
        out[wide : wide + half, 0:64] = acc[0:half, 128:192]
        out[wide : wide + half, 64:128] = acc[half:wide, 128:192]
        out[wide + half :, :] = small[...]


def backward_kernel(dpre, top, bot, side, w, out, bordered, turned, *, rows):
    step = pl.program_id(0)
    channels = w.shape[0]

    def place(i, row):
        bordered[i] = shifted(row.astype(F32), side[i].astype(F32))

    @pl.when(step == 0)
    def _():
        for ii in range(DIL):
            place(ii, top[ii])
            place(ii + DIL, dpre[ii])

    @pl.when((step > 0) & (step < pl.num_programs(0) - 1))
    def _():
        for ii in range(8):
            i = step * 8 + ii
            place(i, dpre[i - DIL])

    @pl.when(step == pl.num_programs(0) - 1)
    def _():
        for ii in range(DIL):
            place(rows + ii, dpre[rows - DIL + ii])
            place(rows + DIL + ii, bot[ii])

    @pl.when(step > 0)
    def _():
        for ii in range(8):
            i = (step - 1) * 8 + ii
            window = jnp.concatenate([bordered[i + DIL * a] for a in range(3)], axis=0)
            put(turned, ii, 8, jnp.dot(w[...], window, preferred_element_type=F32))
        for u in range(out.shape[2] // 128):
            at = 8 * channels * u
            block = turned[at : at + 8 * channels, :].reshape(channels, 8, 128)
            out[:, :, 128 * u : 128 * (u + 1)] = block.astype(BF16)


def full(shape):
    return pl.BlockSpec(shape, lambda *_: (0,) * len(shape))


def total_over_tiles(value):
    for axis in ("col", "row"):
        count = lax.axis_size(axis)
        if count & (count - 1):
            value = lax.psum(value, axis)
            continue
        bit = 1
        while bit < count:
            value = value + lax.ppermute(value, axis, [(i, i ^ bit) for i in range(count)])
            bit *= 2
    return value


def per_device(x, labels, lengths, conv_weight, conv_bias, head_weight, head_bias):
    channels, rows, width = x.shape
    nbins = head_weight.shape[0]
    nrow, ncol = lax.axis_size("row"), lax.axis_size("col")
    q = width // rows
    assert rows == 64 and q * rows == width and q & (q - 1) == 0 and q * ncol == nrow
    nb = -(-nbins // 8) * 8
    pairs = (nbins + 1) // 2
    high = rows + 2 * DIL
    groups = rows // 8
    tiles = width // 128
    r, c = lax.axis_index("row"), lax.axis_index("col")
    limit = pltpu.CompilerParams(vmem_limit_bytes=56 * 1024 * 1024)

    scal = jnp.stack([r % q, r * rows, c * width, lengths[0]]).astype(jnp.int32)
    w_fwd = conv_weight.transpose(2, 0, 1, 3).reshape(channels, 9 * channels)
    w_bwd = conv_weight[::-1, ::-1].transpose(3, 0, 1, 2).reshape(channels, 9 * channels)
    hw = jnp.pad(head_weight, ((0, nb - nbins), (0, 0)))

    top, bot = row_exchange(x[:, :DIL, :], x[:, rows - DIL :, :])
    tall = [top, x, bot]
    to_left = jnp.concatenate([v[:, :, :DIL] for v in tall], axis=1)
    to_right = jnp.concatenate([v[:, :, width - DIL :] for v in tall], axis=1)
    flat = (channels, high * DIL)
    left, right = col_exchange(to_left.reshape(flat), to_right.reshape(flat))
    side = side_lanes(
        left.reshape(channels, high, DIL), right.reshape(channels, high, DIL)
    )

    band = labels.shape[0]
    mine = labels.astype(BF16).reshape(band, ncol, width)
    strips = jnp.zeros((ncol, band, width), BF16)
    for d in range(ncol):
        piece = lax.dynamic_index_in_dim(mine, (c + d) % ncol, axis=1, keepdims=False)
        if d:
            piece = lax.ppermute(piece, "col", [(i, (i + d) % ncol) for i in range(ncol)])
        strips = lax.dynamic_update_index_in_dim(strips, piece, (c - d) % ncol, axis=0)
    tile_labels = strips.reshape(rows, width).astype(jnp.int32)

    outs = pl.pallas_call(
        functools.partial(forward_kernel, rows=rows, q=q),
        grid_spec=pltpu.PrefetchScalarGridSpec(
            num_scalar_prefetch=1,
            grid=(groups + 1,),
            in_specs=[
                full((channels, rows, width)),
                full((channels, DIL, width)),
                full((channels, DIL, width)),
                full((channels, high, 128)),
                full((channels, 9 * channels)),
                full((channels, 1)),
                full((nb, channels)),
            ],
            out_specs=[
                pl.BlockSpec((8, 3 * channels, width), lambda g, s: (g, 0, 0)),
                pl.BlockSpec((8, channels, width), lambda g, s: (jnp.maximum(g - 1, 0), 0, 0)),
                pl.BlockSpec((8, channels, width), lambda g, s: (jnp.maximum(g - 1, 0), 0, 0)),
                full((tiles * nb * rows, 128)),
            ]
            + [full((pairs, rows, 128))] * q,
            scratch_shapes=[
                pltpu.VMEM((tiles * channels * high, 128), F32),
                pltpu.VMEM((channels * high, 128), F32),
                pltpu.VMEM((high, 3 * channels, width), BF16),
                pltpu.VMEM((q, pairs, rows, 128), BF16),
            ],
        ),
        out_shape=[
            jax.ShapeDtypeStruct((high, 3 * channels, width), BF16),
            jax.ShapeDtypeStruct((rows, channels, width), BF16),
            jax.ShapeDtypeStruct((rows, channels, width), BF16),
            jax.ShapeDtypeStruct((tiles * nb * rows, 128), F32),
        ]
        + [jax.ShapeDtypeStruct((pairs, rows, 128), BF16)] * q,
        compiler_params=limit,
        name="forward",
    )(scal, x, top, bot, side, w_fwd, conv_bias[:, None], hw)
    xs, hid, slope, direct = outs[:4]

    got = []
    for t in range(q):
        perm = [
            (i * ncol + j, (q * j + (i % q ^ t)) * ncol + i // q)
            for i in range(nrow)
            for j in range(ncol)
        ]
        got.append(lax.ppermute(outs[4 + t], ROWS, perm))

    dpre, small = pl.pallas_call(
        functools.partial(middle_kernel, q=q, nbins=nbins),
        grid_spec=pltpu.PrefetchScalarGridSpec(
            num_scalar_prefetch=2,
            grid=(groups,),
            in_specs=[
                pl.BlockSpec((tiles, nb, 8, 128), lambda g, *_: (0, 0, g, 0)),
                pl.BlockSpec((8, width), lambda g, *_: (g, 0)),
                pl.BlockSpec((8, channels, width), lambda g, *_: (g, 0, 0)),
                pl.BlockSpec((8, channels, width), lambda g, *_: (g, 0, 0)),
                full((channels, nb)),
            ]
            + [pl.BlockSpec((pairs, 8, 128), lambda g, *_: (0, g, 0))] * q,
            out_specs=[
                pl.BlockSpec((8, channels, width), lambda g, *_: (g, 0, 0)),
                full((channels, 128)),
            ],
            scratch_shapes=[
                pltpu.VMEM((tiles * nb * 8, 128), F32),
                pltpu.VMEM((channels, 128), F32),
                pltpu.VMEM((nb * 8, 128), F32),
                pltpu.VMEM((channels, width), F32),
                pltpu.VMEM((8, 128), F32),
            ],
        ),
        out_shape=[
            jax.ShapeDtypeStruct((rows, channels, width), BF16),
            jax.ShapeDtypeStruct((channels, 128), F32),
        ],
        compiler_params=limit,
        name="middle",
    )(scal, head_bias, direct.reshape(tiles, nb, rows, 128), tile_labels, hid, slope, hw.T, *got)

    above, below = row_exchange(dpre[:DIL], dpre[rows - DIL :])
    tall = [above, dpre, below]
    to_left = jnp.concatenate([v[:, :, :DIL] for v in tall], axis=0)
    to_right = jnp.concatenate([v[:, :, width - DIL :] for v in tall], axis=0)
    flat = (high, channels * DIL)
    left, right = col_exchange(to_left.reshape(flat), to_right.reshape(flat))
    side = side_lanes(
        left.reshape(high, channels, DIL), right.reshape(high, channels, DIL)
    )

    wide = 3 * channels
    sums = pl.pallas_call(
        functools.partial(weight_kernel, rows=rows),
        grid=(groups + 1,),
        in_specs=[
            pl.BlockSpec((8, wide, width), lambda g: (g, 0, 0)),
            full((rows, channels, width)),
            full((channels, 128)),
        ],
        out_specs=full((wide + wide // 2 + channels, 128)),
        out_shape=jax.ShapeDtypeStruct((wide + wide // 2 + channels, 128), F32),
        scratch_shapes=[
            pltpu.VMEM((wide, wide), F32),
            pltpu.VMEM((rows + 16, channels, width), BF16),
        ],
        compiler_params=limit,
        name="weights",
    )(xs, dpre, small)
    sums = total_over_tiles(sums)

    pair_gradient = pl.pallas_call(
        functools.partial(backward_kernel, rows=rows),
        grid=(groups + 1,),
        in_specs=[
            full((rows, channels, width)),
            full((DIL, channels, width)),
            full((DIL, channels, width)),
            full((high, channels, 128)),
            full((channels, 9 * channels)),
        ],
        out_specs=pl.BlockSpec(
            (channels, 8, width), lambda g: (0, jnp.maximum(g - 1, 0), 0)
        ),
        out_shape=jax.ShapeDtypeStruct((channels, rows, width), BF16),
        scratch_shapes=[
            pltpu.VMEM((high, wide, width), BF16),
            pltpu.VMEM((tiles * channels * 8, 128), F32),
        ],
        compiler_params=limit,
        name="backward",
    )(dpre, above, below, side, w_bwd)

    half = wide // 2
    tail = sums[wide : wide + half]
    taps = jnp.concatenate(
        [sums[:wide], jnp.concatenate([tail[:, :64], tail[:, 64:]], axis=0)], axis=1
    )
    conv_grad = taps.reshape(3, channels, 3, channels).transpose(0, 2, 1, 3)
    rest = sums[wide + half :]
    area = (lengths[0] * lengths[0]).astype(F32)
    return (
        pair_gradient,
        conv_grad,
        rest[:, channels + 1],
        rest[:nbins, :channels],
        rest[:nbins, channels],
        (rest[0, channels + 2] / area).reshape(1),
    )


def solution(mesh):
    return jax.shard_map(
        per_device,
        mesh=mesh,
        in_specs=(
            P(None, ("parts", "row"), "col"),
            P(("parts", "row", "col"), None),
            P("parts"),
            P(),
            P(),
            P(),
            P(),
        ),
        out_specs=(
            P(None, ("parts", "row"), "col"),
            P("parts", None, None, None),
            P("parts"),
            P("parts", None),
            P("parts"),
            P("parts"),
        ),
        check_vma=False,
    )
```

```python
import functools

import jax
import jax.numpy as jnp
from jax import lax
from jax.experimental import pallas as pl
from jax.experimental.pallas import tpu as pltpu
from jax.sharding import PartitionSpec as P

DIL = 4
ROWS = ("row", "col")
F32 = jnp.float32
BF16 = jnp.bfloat16
VM = pl.BlockSpec(memory_space=pltpu.VMEM)
SM = pl.BlockSpec(memory_space=pltpu.SMEM)
MIB = 1024 * 1024


def grant(mib):
    return pltpu.CompilerParams(vmem_limit_bytes=mib * MIB)


def cost(us):
    return pl.CostEstimate(flops=int(us * 1.1e9), transcendentals=0, bytes_accessed=0)


def call(body, name, out_shape, args, us, smem=0, scratch=(), aliases=None, mib=4):
    return pl.pallas_call(
        body,
        out_shape=out_shape,
        in_specs=[SM] * smem + [VM] * (len(args) - smem),
        out_specs=jax.tree.map(lambda _: VM, out_shape),
        scratch_shapes=list(scratch),
        input_output_aliases=aliases or {},
        compiler_params=grant(mib),
        cost_estimate=cost(us),
        name=name,
    )(*args)


def shape(dims, dtype=BF16):
    return jax.ShapeDtypeStruct(dims, dtype)


def pairs_of(tiles):
    return jnp.concatenate(tiles, axis=1)


def prep_kernel(x, out, head, tail, main):
    some, rows, width = x.shape
    tiles, _, channels, _ = out.shape
    step = pl.program_id(0)

    for cc in range(some):
        body = x[cc].astype(F32)
        for u in range(tiles):
            at = pl.multiple_of((u * channels + step * some + cc) * rows, 8)
            main[pl.ds(at, rows), :] = body[:, 128 * u : 128 * (u + 1)]

    @pl.when(step == pl.num_programs(0) - 1)
    def _():
        def turn(i, _):
            for u in range(tiles):
                at = u * channels * rows + i
                out[u, i] = main[pl.ds(at, channels, stride=rows), :].astype(BF16)
            return 0

        lax.fori_loop(0, rows, turn, 0, unroll=8)
        for u in range(tiles):
            head[u] = out[u, :DIL]
            tail[u] = out[u, rows - DIL :]


def edges_kernel(scal, field, above, below, *sides, ncol):
    tiles, rows, channels, _ = field.shape
    lane = lax.broadcasted_iota(jnp.int32, (channels, 128), 1) // DIL
    if ncol == 2:
        first = scal[4] == 0
        picks = [(jnp.where(first, tiles - 1, 0), jnp.where(first, DIL, 0))]
    else:
        picks = [(0, 0), (tiles - 1, DIL)]
    per = 128 // DIL
    for (tile, extra), out in zip(picks, sides):

        def add(slot, row, acc):
            moved = pltpu.roll(row.astype(F32), lax.rem(slot * DIL + extra, 128), 1)
            return jnp.where(lane == slot, moved, acc)

        for part in range(out.shape[0]):
            acc = jnp.zeros((channels, 128), F32)
            start = part * per - DIL
            if part == 0:
                for ii in range(DIL):
                    acc = add(ii, above[tile, ii], acc)
                start = 0
            stop = min((part + 1) * per - DIL, rows)

            def body(i, acc):
                return add(i + DIL - part * per, field[tile, i], acc)

            acc = lax.fori_loop(start, stop, body, acc, unroll=4)
            if part == out.shape[0] - 1:
                for ii in range(DIL):
                    acc = add(rows + DIL + ii - part * per, below[tile, ii], acc)
            out[part] = acc.astype(BF16)


def border_kernel(scal, field, above, below, *rest, ncol):
    sides, (out, lefts, rights) = rest[:-3], rest[-3:]
    tiles, rows, channels, _ = field.shape
    for p in range(lefts.shape[0]):
        if ncol == 2:
            first = scal[4] == 0
            v = sides[0][p].astype(F32)
            lefts[p] = jnp.where(first, 0.0, v)
            rights[p] = jnp.where(first, v, 0.0)
        else:
            lefts[p] = sides[0][p].astype(F32)
            rights[p] = sides[1][p].astype(F32)
    lane = lax.broadcasted_iota(jnp.int32, (channels, 128), 1)
    per = 128 // DIL

    def place(i, row):
        part, at = i // per, lax.rem(i, per) * DIL
        left = pltpu.roll(lefts[part], lax.rem(128 - at, 128), 1)
        right = pltpu.roll(rights[part], lax.rem(256 - DIL - at, 128), 1)
        row = [v.astype(F32) for v in row]
        whole = pairs_of(row)
        before = pltpu.roll(whole, DIL, 1)
        after = pltpu.roll(whole, whole.shape[1] - DIL, 1)
        for u in range(tiles):
            b = before[:, 128 * u : 128 * (u + 1)]
            a = after[:, 128 * u : 128 * (u + 1)]
            if u == 0:
                b = jnp.where(lane < DIL, left, b)
            if u == tiles - 1:
                a = jnp.where(lane >= 128 - DIL, right, a)
            out[u, i] = jnp.concatenate(
                [b.astype(BF16), row[u].astype(BF16), a.astype(BF16)], axis=0
            )

    for i in range(DIL):
        place(i, [above[u, i] for u in range(tiles)])
        place(i + rows + DIL, [below[u, i] for u in range(tiles)])

    def body(i, _):
        place(i + DIL, [field[u, i] for u in range(tiles)])
        return 0

    lax.fori_loop(0, rows, body, 0, unroll=4)


def forward_kernel(scal, xs, w, bias, hw, hid, slope, direct, one, two, *, stage):
    rows, channels, _ = hid.shape
    nb = hw.shape[0]
    rq = scal[0]
    u = (rq >> 1) ^ stage

    def window(i):
        return jnp.concatenate([xs[u, i + DIL * a] for a in range(3)], axis=0)

    def conv(g, _):
        for p in range(4):
            i = g * 8 + 2 * p
            pre = jnp.dot(
                w[...], pairs_of([window(i), window(i + 1)]), preferred_element_type=F32
            )
            pre = pre + bias[...]
            grown = jnp.exp(jnp.minimum(pre, 0.0))
            h = jnp.where(pre > 0, pre, grown - 1.0).astype(BF16)
            s = jnp.where(pre > 0, 1.0, grown).astype(BF16)
            for e in range(2):
                hid[i + e] = h[:, 128 * e : 128 * (e + 1)]
                slope[i + e] = s[:, 128 * e : 128 * (e + 1)]
        return 0

    lax.fori_loop(0, rows // 8, conv, 0)

    def head(g, _):
        for p in range(4):
            i = g * 8 + 2 * p
            d = jnp.dot(hw[...], pairs_of([hid[i], hid[i + 1]]), preferred_element_type=F32)
            for e in range(2):
                direct[pl.ds(i + e, nb, stride=rows), :] = d[:, 128 * e : 128 * (e + 1)]
        return 0

    lax.fori_loop(0, rows // 8, head, 0)

    flip = (rq & 1) == 1
    for m in range(one.shape[0]):
        turned = direct[2 * rows * m : 2 * rows * (m + 1), :].T.astype(BF16)
        low, high = turned[:rows].astype(F32), turned[rows:].astype(F32)
        one[m] = jnp.where(flip, high, low).astype(BF16)
        two[m] = jnp.where(flip, low, high).astype(BF16)


def middle_kernel(scal, hb, direct, labels, hid, slope, hwt, one, two, *rest, stage, last, nbins):
    if stage:
        before, rest = rest[1], rest[2:]
    dpre, small, *ends, dl, hacc, bacc, cacc, lacc = rest
    nb, rows, _ = direct.shape
    channels = hwt.shape[0]
    rq, extent = scal[0], scal[3]
    u = (rq >> 1) ^ stage
    flip = (rq & 1) == 1
    for ref in (hacc, bacc, cacc, lacc):
        ref[...] = jnp.zeros_like(ref)
    dl[nbins * rows :, :] = jnp.zeros((dl.shape[0] - nbins * rows, 128), F32)

    lane = lax.broadcasted_iota(jnp.int32, (8, 128), 1)
    low = lane < 64
    col_ids = scal[2] + 128 * u + lane
    area = (extent * extent).astype(F32)

    def softmax(g, _):
        base = pl.multiple_of(g * 8, 8)
        row_ids = scal[1] + base + lax.broadcasted_iota(jnp.int32, (8, 128), 0)
        valid = jnp.where((row_ids < extent) & (col_ids < extent), 1.0, 0.0)
        wanted = labels[u, pl.ds(base, 8), :]
        logits = []
        for m in range((nbins + 1) // 2):
            a = one[m, pl.ds(base, 8), :].astype(F32)
            b = two[m, pl.ds(base, 8), :].astype(F32)
            a, b = jnp.where(flip, b, a), jnp.where(flip, a, b)
            mirror = (
                jnp.where(low, a, pltpu.roll(b, 64, 1)),
                jnp.where(low, pltpu.roll(a, 64, 1), b),
            )
            for k in range(2 * m, min(2 * m + 2, nbins)):
                logits.append(
                    0.5 * (direct[k, pl.ds(base, 8), :] + mirror[k - 2 * m]) + hb[k]
                )
        peak = functools.reduce(jnp.maximum, logits)
        picked = functools.reduce(
            lambda a, b: a + b,
            [jnp.where(wanted == k, logits[k], 0.0) for k in range(nbins)],
        )
        powers = [jnp.exp(v - peak) for v in logits]
        total = functools.reduce(lambda a, b: a + b, powers)
        lacc[...] += valid * (peak + jnp.log(total) - picked)
        inverse = 1.0 / total
        scale = valid / area
        for k in range(nbins):
            d = (powers[k] * inverse - jnp.where(wanted == k, 1.0, 0.0)) * scale
            d = d.astype(BF16).astype(F32)
            dl[pl.ds(k * rows + base, 8), :] = d
            bacc[8 * k : 8 * k + 8, :] += d
        return 0

    lax.fori_loop(0, rows // 8, softmax, 0)

    def back(g, _):
        for p in range(4):
            i = g * 8 + 2 * p
            d = pairs_of(
                [dl[pl.ds(i + e, nb, stride=rows), :].astype(BF16) for e in range(2)]
            )
            h = pairs_of([hid[i], hid[i + 1]])
            s = pairs_of([slope[i], slope[i + 1]])
            v = jnp.dot(hwt[...], d, preferred_element_type=F32) * s.astype(F32)
            v = v.astype(BF16)
            dpre[u, i] = v[:, :128]
            dpre[u, i + 1] = v[:, 128:]
            cacc[...] += v[:, :128].astype(F32) + v[:, 128:].astype(F32)
            hacc[0:nb, 0:channels] += lax.dot_general(
                d, h, (((1,), (1,)), ((), ())), preferred_element_type=F32
            )
        return 0

    lax.fori_loop(0, rows // 8, back, 0)

    spot = lax.broadcasted_iota(jnp.int32, small.shape, 1)
    sums = jnp.sum(bacc[...].reshape(nb, 8, 128), axis=1)
    sums = jnp.sum(sums, axis=1, keepdims=True)
    sums = jnp.concatenate([sums, jnp.zeros((channels - nb, 1), F32)], axis=0)
    biases = jnp.sum(cacc[...], axis=1, keepdims=True)
    loss = jnp.sum(jnp.sum(lacc[...], axis=1, keepdims=True), axis=0, keepdims=True)
    value = jnp.where(
        spot < channels,
        hacc[...],
        jnp.where(spot == channels, sums, jnp.where(spot == channels + 1, biases, loss)),
    )
    small[...] = value + before[...] if stage else value
    if last:
        for v in range(dpre.shape[0]):
            ends[0][v] = dpre[v, :DIL]
            ends[1][v] = dpre[v, rows - DIL :]


def weight_kernel(xs, dpre, small, out, acc, padded):
    tiles, rows, channels, _ = dpre.shape
    wide = 3 * channels
    acc[...] = jnp.zeros_like(acc)
    for u in range(tiles):
        padded[u, 0:8] = jnp.zeros((8, channels, 128), BF16)
        padded[u, 8 : 8 + rows] = dpre[u]
        padded[u, 8 + rows : 16 + rows] = jnp.zeros((8, channels, 128), BF16)

    def body(g, _):
        left, right = [], []
        for ii in range(8):
            i = g * 8 + ii
            for u in range(tiles):
                left.append(
                    jnp.concatenate([padded[u, i + 8 - DIL * a] for a in range(3)], axis=0)
                )
                right.append(xs[u, i])
        acc[...] += lax.dot_general(
            pairs_of(left), pairs_of(right), (((1,), (1,)), ((), ())),
            preferred_element_type=F32,
        )
        return 0

    lax.fori_loop(0, rows // 8 + 1, body, 0)
    half = wide // 2
    out[0:wide, :] = acc[:, 0:128]
    out[wide : wide + half, 0:64] = acc[0:half, 128:192]
    out[wide : wide + half, 64:128] = acc[half:wide, 128:192]
    out[wide + half :, :] = small[...]


def backward_kernel(ds, w, out, turned):
    step = pl.program_id(0)
    channels, _, width = out.shape
    tiles = width // 128
    for ii in range(8):
        i = step * 8 + ii
        window = pairs_of(
            [
                jnp.concatenate([ds[u, i + DIL * a] for a in range(3)], axis=0)
                for u in range(tiles)
            ]
        )
        v = jnp.dot(w[...], window, preferred_element_type=F32)
        for u in range(tiles):
            turned[pl.ds(u * channels * 8 + ii, channels, stride=8), :] = v[
                :, 128 * u : 128 * (u + 1)
            ]
    for u in range(tiles):
        at = 8 * channels * u
        block = turned[at : at + 8 * channels, :].reshape(channels, 8, 128)
        out[:, :, 128 * u : 128 * (u + 1)] = block.astype(BF16)


def side_columns(field, above, below, scal):
    parts = -(-(field.shape[1] + 2 * DIL) * DIL // 128)
    ncol = lax.axis_size("col")
    return call(
        functools.partial(edges_kernel, ncol=ncol),
        "edges",
        [shape((parts, field.shape[2], 128))] * (1 if ncol == 2 else 2),
        (scal, field, above, below),
        us=1.5,
        smem=1,
    )


def with_border(field, above, below, sides, scal):
    tiles, rows, channels, _ = field.shape
    ncol = lax.axis_size("col")
    if ncol == 2:
        got = [lax.ppermute(sides[0], "col", [(0, 1), (1, 0)])]
    else:
        to_left, to_right = sides
        got = [
            lax.ppermute(to_right, "col", [(i, i + 1) for i in range(ncol - 1)]),
            lax.ppermute(to_left, "col", [(i + 1, i) for i in range(ncol - 1)]),
        ]
    return call(
        functools.partial(border_kernel, ncol=ncol),
        "border",
        shape((tiles, rows + 2 * DIL, 3 * channels, 128)),
        (scal, field, above, below, *got),
        us=4,
        smem=1,
        scratch=[pltpu.VMEM(got[0].shape, F32)] * 2,
    )


def row_halo(head, tail):
    count = lax.axis_size("row")
    above = lax.ppermute(tail, "row", [(i, i + 1) for i in range(count - 1)])
    below = lax.ppermute(head, "row", [(i + 1, i) for i in range(count - 1)])
    return above, below


def total_over_tiles(value):
    nrow, ncol = lax.axis_size("row"), lax.axis_size("col")
    if ncol == 2 and nrow % 2 == 0 and nrow <= 8 and value.shape[0] % 32 == 0:
        r, c = lax.axis_index("row"), lax.axis_index("col")
        me = (r % 2) * 2 + c
        parts = value.reshape(4, value.shape[0] // 4, value.shape[1])

        def near(v, d):
            perm = [
                (i * 2 + j, (i ^ (d >> 1)) * 2 + (j ^ (d & 1)))
                for i in range(nrow)
                for j in range(2)
            ]
            return lax.ppermute(v, ROWS, perm)

        own = lax.dynamic_index_in_dim(parts, me, 0, False)
        for d in (1, 2, 3):
            own = own + near(lax.dynamic_index_in_dim(parts, me ^ d, 0, False), d)
        summed = own
        for d in range(1, nrow // 2):
            perm = [(i, (i + 2 * d) % nrow) for i in range(nrow)]
            summed = summed + lax.ppermute(own, "row", perm)
        got = [summed] + [near(summed, d) for d in (1, 2, 3)]
        return got, jnp.stack([me, me ^ 1, me ^ 2, me ^ 3]).astype(jnp.int32)
    for axis, count in (("col", ncol), ("row", nrow)):
        if count & (count - 1):
            value = lax.psum(value, axis)
            continue
        bit = 1
        while bit < count:
            value = value + lax.ppermute(value, axis, [(i, i ^ bit) for i in range(count)])
            bit *= 2
    return [value], jnp.zeros((1,), jnp.int32)


def unpack_kernel(where, extent, *rest):
    parts, (taps, biases, heads, head_biases, loss, buf) = rest[:-6], rest[-6:]
    for n, part in enumerate(parts):
        size = part.shape[0]
        buf[pl.ds(pl.multiple_of(where[n] * size, 8), size), :] = part[...]
    ch = taps.shape[2]
    half = 3 * ch // 2
    for a in range(3):
        taps[a, 0] = buf[a * ch : (a + 1) * ch, 0:ch]
        taps[a, 1] = buf[a * ch : (a + 1) * ch, ch : 2 * ch]
        for o in range(0, ch, 32):
            at = a * ch + o
            lanes = slice(0, ch) if at < half else slice(ch, 2 * ch)
            row = 3 * ch + at % half
            taps[a, 2, o : o + 32] = buf[row : row + 32, lanes]
    small = buf[3 * ch + half :, :]
    turned = small.T
    heads[...] = small[: heads.shape[0], :ch]
    head_biases[...] = turned[ch : ch + 1, : heads.shape[0]]
    biases[...] = turned[ch + 1 : ch + 2, :]
    area = (extent[0] * extent[0]).astype(F32)
    loss[...] = turned[ch + 2 : ch + 3, 0:1] / area


def per_device(x, labels, lengths, conv_weight, conv_bias, head_weight, head_bias):
    channels, rows, width = x.shape
    nbins = head_weight.shape[0]
    nrow, ncol = lax.axis_size("row"), lax.axis_size("col")
    q = width // rows
    tiles = width // 128
    assert rows == 64 and channels == 64 and q == 2 * tiles and q & (q - 1) == 0
    assert q * ncol == nrow and 128 * tiles == width
    nb = -(-nbins // 8) * 8
    pairs = (nbins + 1) // 2
    wide = 3 * channels
    r, c = lax.axis_index("row"), lax.axis_index("col")

    scal = jnp.stack([r % q, r * rows, c * width, lengths[0], c]).astype(jnp.int32)
    w_fwd = conv_weight.transpose(2, 0, 1, 3).reshape(channels, 9 * channels)
    w_bwd = conv_weight[::-1, ::-1].transpose(3, 0, 1, 2).reshape(channels, 9 * channels)
    hw = jnp.pad(head_weight, ((0, nb - nbins), (0, 0)))

    field = (tiles, rows, channels, 128)
    strip = (tiles, DIL, channels, 128)
    xt, head, tail = pl.pallas_call(
        prep_kernel,
        grid=(channels // 8,),
        in_specs=[pl.BlockSpec((8, rows, width), lambda g: (g, 0, 0))],
        out_specs=[VM, VM, VM],
        out_shape=[shape(field), shape(strip), shape(strip)],
        scratch_shapes=[pltpu.VMEM((tiles * channels * rows, 128), F32)],
        compiler_params=grant(8),
        cost_estimate=cost(4),
        name="prep",
    )(x)
    above, below = row_halo(head, tail)
    xs = with_border(xt, above, below, side_columns(xt, above, below, scal), scal)

    band = labels.shape[0]
    mine = labels.astype(BF16).reshape(band, ncol, width)
    strips = jnp.zeros((ncol, band, width), BF16)
    for d in range(ncol):
        piece = lax.dynamic_index_in_dim(mine, (c + d) % ncol, axis=1, keepdims=False)
        if d:
            piece = lax.ppermute(piece, "col", [(i, (i + d) % ncol) for i in range(ncol)])
        strips = lax.dynamic_update_index_in_dim(strips, piece, (c - d) % ncol, axis=0)
    tile_labels = strips.reshape(rows, tiles, 128).transpose(1, 0, 2).astype(jnp.int32)

    kept, got = [], []
    for stage in range(tiles):
        block = shape((pairs, rows, 128))
        hid, slope, direct, *sends = call(
            functools.partial(forward_kernel, stage=stage),
            "forward",
            [shape(field[1:]), shape(field[1:]), shape((nb * rows, 128), F32), block, block],
            (scal, xs, w_fwd, conv_bias[:, None], hw),
            us=6,
            smem=1,
        )
        kept.append((hid, slope, direct))
        for e in range(2):
            t = 2 * stage + e
            perm = [
                (i * ncol + j, (q * j + (i % q ^ t)) * ncol + i // q)
                for i in range(nrow)
                for j in range(ncol)
            ]
            got.append(lax.ppermute(sends[e], ROWS, perm))

    dpre = small = ends = None
    for stage in range(tiles):
        hid, slope, direct = kept[stage]
        args = (
            scal,
            head_bias,
            direct.reshape(nb, rows, 128),
            tile_labels,
            hid,
            slope,
            hw.T,
            got[2 * stage],
            got[2 * stage + 1],
        )
        last = stage == tiles - 1
        dpre, small, *ends = call(
            functools.partial(middle_kernel, stage=stage, last=last, nbins=nbins),
            "middle",
            [shape(field), shape((channels, 128), F32)] + [shape(strip)] * (2 * last),
            args + ((dpre, small) if stage else ()),
            us=5,
            smem=2,
            scratch=[
                pltpu.VMEM((nb * rows, 128), F32),
                pltpu.VMEM((channels, 128), F32),
                pltpu.VMEM((nb * 8, 128), F32),
                pltpu.VMEM((channels, 128), F32),
                pltpu.VMEM((8, 128), F32),
            ],
            aliases={len(args): 0} if stage else None,
        )

    sums = call(
        weight_kernel,
        "weights",
        shape((wide + wide // 2 + channels, 128), F32),
        (xs, dpre, small),
        us=4,
        mib=8,
        scratch=[
            pltpu.VMEM((wide, wide), F32),
            pltpu.VMEM((tiles, rows + 16, channels, 128), BF16),
        ],
    )
    above, below = row_halo(*ends)
    sides = side_columns(dpre, above, below, scal)
    sides, sums = lax.optimization_barrier((sides, sums))
    ds = with_border(dpre, above, below, sides, scal)
    parts, where = total_over_tiles(sums)

    pair_gradient = pl.pallas_call(
        backward_kernel,
        grid=(rows // 8,),
        in_specs=[VM, VM],
        out_specs=pl.BlockSpec((channels, 8, width), lambda g: (0, g, 0)),
        out_shape=shape((channels, rows, width)),
        scratch_shapes=[pltpu.VMEM((tiles * channels * 8, 128), F32)],
        compiler_params=grant(8),
        cost_estimate=cost(6),
        name="backward",
    )(ds, w_bwd)

    conv_grad, biases, heads, head_biases, loss = pl.pallas_call(
        unpack_kernel,
        in_specs=[SM, SM] + [VM] * len(parts),
        out_shape=[
            shape((3, 3, channels, channels), F32),
            shape((1, channels), F32),
            shape((nbins, channels), F32),
            shape((1, nbins), F32),
            shape((1, 1), F32),
        ],
        scratch_shapes=[pltpu.VMEM(sums.shape, F32)],
        compiler_params=grant(4),
        cost_estimate=cost(1),
        name="unpack",
    )(where, lengths, *parts)
    return (
        pair_gradient,
        conv_grad,
        biases.reshape(channels),
        heads,
        head_biases.reshape(nbins),
        loss.reshape(1),
    )


def solution(mesh):
    return jax.shard_map(
        per_device,
        mesh=mesh,
        in_specs=(
            P(None, ("parts", "row"), "col"),
            P(("parts", "row", "col"), None),
            P("parts"),
            P(),
            P(),
            P(),
            P(),
        ),
        out_specs=(
            P(None, ("parts", "row"), "col"),
            P("parts", None, None, None),
            P("parts"),
            P("parts", None),
            P("parts"),
            P("parts"),
        ),
        check_vma=False,
    )
```

```python
import functools

import jax
import jax.numpy as jnp
from jax import lax
from jax.experimental import pallas as pl
from jax.experimental.pallas import tpu as pltpu
from jax.sharding import PartitionSpec as P

DIL = 4
ROWS = ("row", "col")
F32 = jnp.float32
BF16 = jnp.bfloat16
VM = pl.BlockSpec(memory_space=pltpu.VMEM)
SM = pl.BlockSpec(memory_space=pltpu.SMEM)
MIB = 1024 * 1024


def grant(mib):
    return pltpu.CompilerParams(vmem_limit_bytes=mib * MIB)


def cost(us):
    return pl.CostEstimate(flops=int(us * 1.1e9), transcendentals=0, bytes_accessed=0)


def call(body, name, out_shape, args, us, smem=0, scratch=(), aliases=None, mib=4):
    return pl.pallas_call(
        body,
        out_shape=out_shape,
        in_specs=[SM] * smem + [VM] * (len(args) - smem),
        out_specs=jax.tree.map(lambda _: VM, out_shape),
        scratch_shapes=list(scratch),
        input_output_aliases=aliases or {},
        compiler_params=grant(mib),
        cost_estimate=cost(us),
        name=name,
    )(*args)


def shape(dims, dtype=BF16):
    return jax.ShapeDtypeStruct(dims, dtype)


def pairs_of(tiles):
    return jnp.concatenate(tiles, axis=1)


def prep_kernel(_, x, out, head, tail, landed, main, sems):
    channels, rows, width = x.shape
    tiles = width // 128
    some = channels // sems.shape[0]
    copies = [
        pltpu.make_async_copy(
            x.at[pl.ds(n * some, some)], landed.at[pl.ds(n * some, some)], sems.at[n]
        )
        for n in range(sems.shape[0])
    ]
    for copy in copies:
        copy.start()
    for n, copy in enumerate(copies):
        copy.wait()
        for c in range(n * some, (n + 1) * some):
            body = landed[c].astype(F32)
            for u in range(tiles):
                at = (u * channels + c) * rows
                main[at : at + rows, :] = body[:, 128 * u : 128 * (u + 1)]

    def turn(i, _):
        for u in range(tiles):
            at = u * channels * rows + i
            out[u, i] = main[pl.ds(at, channels, stride=rows), :].astype(BF16)
        return 0

    lax.fori_loop(0, rows, turn, 0, unroll=8)
    for u in range(tiles):
        head[u] = out[u, :DIL]
        tail[u] = out[u, rows - DIL :]


def setup_kernel(scal, cw, cb, hw, labels, _, fwd, bwd, bias, head, headt, *pieces):
    ch = cw.shape[2]
    nbins, nb = hw.shape[0], head.shape[0]
    for a in range(3):
        for b in range(3):
            at = (3 * a + b) * ch
            fwd[:, at : at + ch] = cw[a, b]
            bwd[:, at : at + ch] = cw[2 - a, 2 - b].astype(F32).T.astype(BF16)
    bias[...] = jnp.broadcast_to(cb[...], (ch, ch)).T[:, 0:1]
    full = jnp.concatenate([hw[...].astype(F32), jnp.zeros((nb - nbins, ch), F32)], axis=0)
    head[...] = full.astype(BF16)
    headt[...] = full.T.astype(BF16)
    ncol, width = len(pieces), pieces[0].shape[1]
    blocks = [labels[:, width * n : width * (n + 1)] for n in range(ncol)]
    for d, piece in enumerate(pieces):
        want = lax.rem(scal[4] + d, ncol)
        value = blocks[0]
        for n in range(1, ncol):
            value = jnp.where(want == n, blocks[n], value)
        piece[...] = value.astype(F32).astype(BF16)


def edges_kernel(scal, field, above, below, *sides, ncol):
    tiles, rows, channels, _ = field.shape
    lane = lax.broadcasted_iota(jnp.int32, (channels, 128), 1) // DIL
    if ncol == 2:
        first = scal[4] == 0
        picks = [(jnp.where(first, tiles - 1, 0), jnp.where(first, DIL, 0))]
    else:
        picks = [(0, 0), (tiles - 1, DIL)]
    per = 128 // DIL
    for (tile, extra), out in zip(picks, sides):

        def add(slot, row, acc):
            turn = slot * DIL + extra
            turn = turn % 128 if isinstance(turn, int) else lax.rem(turn, 128)
            moved = pltpu.roll(row.astype(F32), turn, 1)
            return jnp.where(lane == slot, moved, acc)

        for part in range(out.shape[0]):
            acc = jnp.zeros((channels, 128), F32)
            start = part * per - DIL
            if part == 0:
                for ii in range(DIL):
                    acc = add(ii, above[tile, ii], acc)
                start = 0
            stop = min((part + 1) * per - DIL, rows)

            def body(i, acc):
                return add(i + DIL - part * per, field[tile, i], acc)

            for i in range(start, stop):
                acc = body(i, acc)
            if part == out.shape[0] - 1:
                for ii in range(DIL):
                    acc = add(rows + DIL + ii - part * per, below[tile, ii], acc)
            out[part] = acc.astype(BF16)


def place(out, i, row):
    tiles = len(row)
    lane = lax.broadcasted_iota(jnp.int32, row[0].shape, 1)
    whole = pairs_of([v.astype(F32) for v in row])
    before = pltpu.roll(whole, DIL, 1)
    after = pltpu.roll(whole, whole.shape[1] - DIL, 1)
    for u in range(tiles):
        b = before[:, 128 * u : 128 * (u + 1)]
        a = after[:, 128 * u : 128 * (u + 1)]
        if u == 0:
            b = jnp.where(lane < DIL, 0.0, b)
        if u == tiles - 1:
            a = jnp.where(lane >= 128 - DIL, 0.0, a)
        out[u, i] = jnp.concatenate([b.astype(BF16), row[u], a.astype(BF16)], axis=0)


def inner_kernel(field, out):
    tiles, rows = field.shape[:2]

    def body(i, _):
        place(out, i + DIL, [field[u, i] for u in range(tiles)])
        return 0

    lax.fori_loop(0, rows, body, 0, unroll=8)


def border_kernel(scal, above, below, *rest, ncol):
    sides, (_, out) = rest[:-2], rest[-2:]
    tiles, high, wide, _ = out.shape
    channels = wide // 3
    for i in range(DIL):
        place(out, i, [above[u, i] for u in range(tiles)])
        place(out, i + high - DIL, [below[u, i] for u in range(tiles)])
    lane = lax.broadcasted_iota(jnp.int32, (channels, 128), 1)
    per = 128 // DIL
    if ncol == 2:
        first = scal[4] == 0
        tile = jnp.where(first, tiles - 1, 0)
        block = pl.multiple_of(jnp.where(first, 2 * channels, 0), channels)
        base = jnp.where(first, 128 - DIL, 0)
        jobs = [(sides[0], tile, block, base)]
    else:
        jobs = [(sides[0], 0, 0, 0), (sides[1], tiles - 1, 2 * channels, 128 - DIL)]
    for side, tile, block, base in jobs:
        mine = (lane >= base) & (lane < base + DIL)
        for part in range(side.shape[0]):

            def patch(ii, _):
                i = part * per + ii
                moved = pltpu.roll(
                    side[part].astype(F32), lax.rem(128 + base - ii * DIL, 128), 1
                )
                spot = (tile, i, pl.ds(block, channels))
                out[spot] = jnp.where(mine, moved, out[spot].astype(F32)).astype(BF16)
                return 0

            lax.fori_loop(0, min(per, high - part * per), patch, 0, unroll=8)


def forward_kernel(scal, xs, w, bias, hw, hid, slope, direct, one, two, *, stage):
    rows, channels, _ = hid.shape
    nb = hw.shape[0]
    rq = scal[0]
    u = (rq >> 1) ^ stage

    def window(i):
        return jnp.concatenate([xs[u, i + DIL * a] for a in range(3)], axis=0)

    def conv(g, _):
        for p in range(4):
            i = g * 8 + 2 * p
            pre = jnp.dot(
                w[...], pairs_of([window(i), window(i + 1)]), preferred_element_type=F32
            )
            pre = pre + bias[...]
            grown = jnp.exp(jnp.minimum(pre, 0.0))
            h = jnp.where(pre > 0, pre, grown - 1.0).astype(BF16)
            s = jnp.where(pre > 0, 1.0, grown).astype(BF16)
            for e in range(2):
                hid[i + e] = h[:, 128 * e : 128 * (e + 1)]
                slope[i + e] = s[:, 128 * e : 128 * (e + 1)]
        return 0

    lax.fori_loop(0, rows // 8, conv, 0)

    def head(g, _):
        for p in range(4):
            i = g * 8 + 2 * p
            d = jnp.dot(hw[...], pairs_of([hid[i], hid[i + 1]]), preferred_element_type=F32)
            for e in range(2):
                direct[pl.ds(i + e, nb, stride=rows), :] = d[:, 128 * e : 128 * (e + 1)]
        return 0

    lax.fori_loop(0, rows // 8, head, 0)

    flip = (rq & 1) == 1
    for m in range(one.shape[0]):
        turned = direct[2 * rows * m : 2 * rows * (m + 1), :].T.astype(BF16)
        low, high = turned[:rows].astype(F32), turned[rows:].astype(F32)
        one[m] = jnp.where(flip, high, low).astype(BF16)
        two[m] = jnp.where(flip, low, high).astype(BF16)


def middle_kernel(scal, hb, direct, hid, slope, hwt, *rest, stage, counts, ncol, first, last, nbins):
    ones, twos, rest = rest[: counts[0]], rest[counts[0] : sum(counts)], rest[sum(counts) :]
    strips, rest = rest[:ncol], rest[ncol:]
    if not first:
        before, rest = rest[1], rest[3:]
    dpre, small, *ends, dl, hacc, bacc, cacc, lacc = rest
    nb, rows, _ = direct.shape
    band = rows // ncol
    channels = hwt.shape[0]
    rq, extent = scal[0], scal[3]
    u = (rq >> 1) ^ stage
    flip = (rq & 1) == 1
    crossed = scal[5] == 1
    for ref in (hacc, bacc, cacc, lacc):
        ref[...] = jnp.zeros_like(ref)
    dl[nbins * rows :, :] = jnp.zeros((dl.shape[0] - nbins * rows, 128), F32)

    lane = lax.broadcasted_iota(jnp.int32, (8, 128), 1)
    low = lane < 64
    col_ids = scal[2] + 128 * u + lane
    area = (extent * extent).astype(F32)

    def softmax(g, _):
        base = pl.multiple_of(g * 8, 8)
        row_ids = scal[1] + base + lax.broadcasted_iota(jnp.int32, (8, 128), 0)
        valid = jnp.where((row_ids < extent) & (col_ids < extent), 1.0, 0.0)
        strip, at = base // band, pl.multiple_of(lax.rem(base, band), 8)
        wanted = jnp.zeros((8, 128), F32)
        for d in range(ncol):
            here = lax.rem(scal[4] + ncol - strip, ncol) == d
            rows8 = strips[d][pl.ds(at, 8), :].astype(F32)
            for v in range(rows8.shape[1] // 128):
                lanes = rows8[:, 128 * v : 128 * (v + 1)]
                wanted = jnp.where(here & (u == v), lanes, wanted)
        logits = []
        for m in range((nbins + 1) // 2):
            a, b = (
                [ref[m, pl.ds(base, 8), :].astype(F32) for ref in refs] for refs in (ones, twos)
            )
            a = a[0] if len(a) == 1 else jnp.where(crossed, a[1], a[0])
            b = b[0] if len(b) == 1 else jnp.where(crossed, b[1], b[0])
            a, b = jnp.where(flip, b, a), jnp.where(flip, a, b)
            mirror = (
                jnp.where(low, a, pltpu.roll(b, 64, 1)),
                jnp.where(low, pltpu.roll(a, 64, 1), b),
            )
            for k in range(2 * m, min(2 * m + 2, nbins)):
                logits.append(
                    0.5 * (direct[k, pl.ds(base, 8), :] + mirror[k - 2 * m]) + hb[k]
                )
        peak = functools.reduce(jnp.maximum, logits)
        picked = functools.reduce(
            lambda a, b: a + b,
            [jnp.where(wanted == k, logits[k], 0.0) for k in range(nbins)],
        )
        powers = [jnp.exp(v - peak) for v in logits]
        total = functools.reduce(lambda a, b: a + b, powers)
        lacc[...] += valid * (peak + jnp.log(total) - picked)
        inverse = 1.0 / total
        scale = valid / area
        for k in range(nbins):
            d = (powers[k] * inverse - jnp.where(wanted == k, 1.0, 0.0)) * scale
            d = d.astype(BF16).astype(F32)
            dl[pl.ds(k * rows + base, 8), :] = d
            bacc[8 * k : 8 * k + 8, :] += d
        return 0

    lax.fori_loop(0, rows // 8, softmax, 0)

    def back(g, _):
        for p in range(4):
            i = g * 8 + 2 * p
            d = pairs_of(
                [dl[pl.ds(i + e, nb, stride=rows), :].astype(BF16) for e in range(2)]
            )
            h = pairs_of([hid[i], hid[i + 1]])
            s = pairs_of([slope[i], slope[i + 1]])
            v = jnp.dot(hwt[...], d, preferred_element_type=F32) * s.astype(F32)
            v = v.astype(BF16)
            dpre[u, i] = v[:, :128]
            dpre[u, i + 1] = v[:, 128:]
            cacc[...] += v[:, :128].astype(F32) + v[:, 128:].astype(F32)
            hacc[0:nb, 0:channels] += lax.dot_general(
                d, h, (((1,), (1,)), ((), ())), preferred_element_type=F32
            )
        return 0

    lax.fori_loop(0, rows // 8, back, 0)

    spot = lax.broadcasted_iota(jnp.int32, small.shape, 1)
    sums = jnp.sum(bacc[...].reshape(nb, 8, 128), axis=1)
    sums = jnp.sum(sums, axis=1, keepdims=True)
    sums = jnp.concatenate([sums, jnp.zeros((channels - nb, 1), F32)], axis=0)
    biases = jnp.sum(cacc[...], axis=1, keepdims=True)
    loss = jnp.sum(jnp.sum(lacc[...], axis=1, keepdims=True), axis=0, keepdims=True)
    value = jnp.where(
        spot < channels,
        hacc[...],
        jnp.where(spot == channels, sums, jnp.where(spot == channels + 1, biases, loss)),
    )
    small[...] = value if first else value + before[...]
    if last:
        for v in range(dpre.shape[0]):
            ends[0][v] = dpre[v, :DIL]
            ends[1][v] = dpre[v, rows - DIL :]


def sum_kernel(*refs):
    refs[-1][...] = functools.reduce(lambda a, b: a + b, [ref[...] for ref in refs[:-1]])


def sum_of(values):
    return call(sum_kernel, "sum", shape(values[0].shape, F32), tuple(values), us=0.5, mib=2)


def weight_kernel(scal, xs, dpre, small, *rest, stage, first):
    if not first:
        before, rest = rest[0], rest[1:]
    padded, outs = rest[-1], rest[:-1]
    _, rows, channels, _ = dpre.shape
    wide = 3 * channels
    u = (scal[0] >> 1) ^ stage
    padded[0:8] = jnp.zeros((8, channels, 128), BF16)
    padded[8 : 8 + rows] = dpre[u]
    padded[8 + rows :] = jnp.zeros((8, channels, 128), BF16)

    def body(g, acc):
        left, right = [], []
        for ii in range(8):
            i = g * 8 + ii
            left.append(
                jnp.concatenate([padded[i + 8 - DIL * a] for a in range(3)], axis=0)
            )
            right.append(xs[u, i])
        acc[...] += lax.dot_general(
            pairs_of(left), pairs_of(right), (((1,), (1,)), ((), ())),
            preferred_element_type=F32,
        )

    acc = outs[-1] if len(outs) == 1 else outs[-2]
    acc[...] = jnp.zeros_like(acc) if first else before[...]
    lax.fori_loop(0, rows // 8 + 1, lambda g, _: body(g, acc), None)
    if len(outs) == 1:
        return
    out, outs = outs[-1], outs[:-2]
    half = wide // 2
    out[0:wide, :] = acc[:, 0:128]
    out[wide : wide + half, 0:64] = acc[0:half, 128:192]
    out[wide : wide + half, 64:128] = acc[half:wide, 128:192]
    out[wide + half :, :] = small[...]
    for n, piece in enumerate(outs):
        size = piece.shape[0]
        piece[...] = out[pl.ds(pl.multiple_of((scal[6] ^ n) * size, 8), size), :]


def backward_kernel(ds, w, out, turned):
    step = pl.program_id(0)
    channels, _, width = out.shape
    tiles = width // 128
    for ii in range(8):
        i = step * 8 + ii
        window = pairs_of(
            [
                jnp.concatenate([ds[u, i + DIL * a] for a in range(3)], axis=0)
                for u in range(tiles)
            ]
        )
        v = jnp.dot(w[...], window, preferred_element_type=F32)
        for u in range(tiles):
            turned[pl.ds(u * channels * 8 + ii, channels, stride=8), :] = v[
                :, 128 * u : 128 * (u + 1)
            ]
    for u in range(tiles):
        at = 8 * channels * u
        block = turned[at : at + 8 * channels, :].reshape(channels, 8, 128)
        out[:, :, 128 * u : 128 * (u + 1)] = block.astype(BF16)


def side_columns(field, above, below, scal):
    parts = -(-(field.shape[1] + 2 * DIL) * DIL // 128)
    ncol = lax.axis_size("col")
    return call(
        functools.partial(edges_kernel, ncol=ncol),
        "edges",
        [shape((parts, field.shape[2], 128))] * (1 if ncol == 2 else 2),
        (scal, field, above, below),
        us=1.5,
        smem=1,
    )


def with_border(inner, above, below, sides, scal):
    ncol = lax.axis_size("col")
    if ncol == 2:
        got = [lax.ppermute(sides[0], "col", [(0, 1), (1, 0)])]
    else:
        to_left, to_right = sides
        got = [
            lax.ppermute(to_right, "col", [(i, i + 1) for i in range(ncol - 1)]),
            lax.ppermute(to_left, "col", [(i + 1, i) for i in range(ncol - 1)]),
        ]
    return call(
        functools.partial(border_kernel, ncol=ncol),
        "border",
        shape(inner.shape),
        (scal, above, below, *got, inner),
        us=1.5,
        smem=1,
        aliases={3 + len(got): 0},
    )


def inner_of(field):
    tiles, rows, channels, _ = field.shape
    return call(
        inner_kernel,
        "inner",
        shape((tiles, rows + 2 * DIL, 3 * channels, 128)),
        (field,),
        us=3,
    )


def row_halo(head, tail):
    count = lax.axis_size("row")
    above = lax.ppermute(tail, "row", [(i, i + 1) for i in range(count - 1)])
    below = lax.ppermute(head, "row", [(i + 1, i) for i in range(count - 1)])
    return above, below


def piece_count(total):
    nrow, ncol = lax.axis_size("row"), lax.axis_size("col")
    return 4 if ncol == 2 and nrow % 2 == 0 and nrow <= 8 and total % 32 == 0 else 1


def total_over_tiles(pieces):
    nrow, ncol = lax.axis_size("row"), lax.axis_size("col")
    if len(pieces) == 4:
        def near(v, d):
            perm = [
                (i * 2 + j, (i ^ (d >> 1)) * 2 + (j ^ (d & 1)))
                for i in range(nrow)
                for j in range(2)
            ]
            return lax.ppermute(v, ROWS, perm)

        own = sum_of([pieces[0]] + [near(pieces[d], d) for d in (1, 2, 3)])
        turns = [[(i, (i + 2 * d) % nrow) for i in range(nrow)] for d in range(1, nrow // 2)]
        own = sum_of([own] + [lax.ppermute(own, "row", turn) for turn in turns])
        return [own] + [near(own, d) for d in (1, 2, 3)]
    value = pieces[0]
    for axis, count in (("col", ncol), ("row", nrow)):
        if count & (count - 1):
            value = lax.psum(value, axis)
            continue
        bit = 1
        while bit < count:
            value = value + lax.ppermute(value, axis, [(i, i ^ bit) for i in range(count)])
            bit *= 2
    return [value]


def unpack_kernel(scal, *rest):
    parts, (taps, biases, heads, head_biases, loss, buf) = rest[:-6], rest[-6:]
    for n, part in enumerate(parts):
        size = part.shape[0]
        buf[pl.ds(pl.multiple_of((scal[6] ^ n) * size, 8), size), :] = part[...]
    ch = taps.shape[2]
    half = 3 * ch // 2
    for a in range(3):
        taps[a, 0] = buf[a * ch : (a + 1) * ch, 0:ch]
        taps[a, 1] = buf[a * ch : (a + 1) * ch, ch : 2 * ch]
        for o in range(0, ch, 32):
            at = a * ch + o
            lanes = slice(0, ch) if at < half else slice(ch, 2 * ch)
            row = 3 * ch + at % half
            taps[a, 2, o : o + 32] = buf[row : row + 32, lanes]
    small = buf[3 * ch + half :, :]
    turned = small.T
    heads[...] = small[: heads.shape[0], :ch]
    head_biases[...] = turned[ch : ch + 1, : heads.shape[0]]
    biases[...] = turned[ch + 1 : ch + 2, :]
    area = (scal[3] * scal[3]).astype(F32)
    loss[...] = turned[ch + 2 : ch + 3, 0:1] / area


def per_device(x, labels, lengths, conv_weight, conv_bias, head_weight, head_bias):
    channels, rows, width = x.shape
    nbins = head_weight.shape[0]
    nrow, ncol = lax.axis_size("row"), lax.axis_size("col")
    q = width // rows
    tiles = width // 128
    assert rows == 64 and channels == 64 and q == 2 * tiles and q & (q - 1) == 0
    assert q * ncol == nrow and 128 * tiles == width
    nb = -(-nbins // 8) * 8
    pairs = (nbins + 1) // 2
    wide = 3 * channels
    total = wide + wide // 2 + channels
    r, c = lax.axis_index("row"), lax.axis_index("col")

    count = piece_count(total)
    mine = (r % 2) * 2 + c if count == 4 else 0 * r
    crossed = (r // q != c).astype(jnp.int32)
    scal = jnp.stack([r % q, r * rows, c * width, lengths[0], c, crossed, mine]).astype(jnp.int32)
    field = (tiles, rows, channels, 128)
    strip = (tiles, DIL, channels, 128)
    xt, head, tail = pl.pallas_call(
        prep_kernel,
        in_specs=[SM, pl.BlockSpec(memory_space=pltpu.HBM)],
        out_specs=[VM, VM, VM],
        out_shape=[shape(field), shape(strip), shape(strip)],
        scratch_shapes=[
            pltpu.VMEM(x.shape, BF16),
            pltpu.VMEM((tiles * channels * rows, 128), F32),
            pltpu.SemaphoreType.DMA((8,)),
        ],
        compiler_params=grant(8),
        cost_estimate=cost(4),
        name="prep",
    )(scal, pltpu.with_memory_space_constraint(x, pltpu.HBM))
    above, below = row_halo(head, tail)
    sides = side_columns(xt, above, below, scal)
    w_fwd, w_bwd, bias, hw, hwt, *mine = call(
        setup_kernel,
        "setup",
        [shape((channels, 9 * channels))] * 2
        + [shape((channels, 1), F32), shape((nb, channels)), shape((channels, nb))]
        + [shape((labels.shape[0], width))] * ncol,
        (scal, conv_weight, conv_bias[None], head_weight, labels, tail),
        us=2,
        smem=1,
    )
    strips = mine[:1] + [
        lax.ppermute(mine[d], "col", [(i, (i + d) % ncol) for i in range(ncol)])
        for d in range(1, ncol)
    ]
    xs = with_border(inner_of(xt), above, below, sides, scal)

    kept, got = [], []
    for stage in range(tiles):
        block = shape((pairs, rows, 128))
        hid, slope, direct, *sends = call(
            functools.partial(forward_kernel, stage=stage),
            "forward",
            [shape(field[1:]), shape(field[1:]), shape((nb * rows, 128), F32), block, block],
            (scal, xs, w_fwd, bias, hw),
            us=6,
            smem=1,
        )
        kept.append((hid, slope, direct))
        for e in range(2):
            t = 2 * stage + e
            perm = [
                (i * ncol + j, (q * j + (i % q ^ t)) * ncol + i // q)
                for i in range(nrow)
                for j in range(ncol)
            ]
            if ncol > 2 or e == 0:
                got.append([lax.ppermute(sends[e], ROWS, perm)])
                continue
            near = [(a, b) for a, b in perm if a % ncol == b % ncol]
            far = [(a, b) for a, b in perm if a % ncol != b % ncol]
            over = [(a, a + b % ncol - a % ncol) for a, b in far]
            along = [(a + b % ncol - a % ncol, b) for a, b in far]
            same = lax.ppermute(sends[e], ROWS, near)
            relayed = lax.ppermute(sends[e], ROWS, over)
            got.append([same, lax.ppermute(relayed, ROWS, along)])

    dpre = small = ends = taps = None
    order = list(range(tiles))
    for stage in order:
        hid, slope, direct = kept[stage]
        ones, twos = got[2 * stage : 2 * stage + 2]
        args = (
            scal,
            head_bias,
            direct.reshape(nb, rows, 128),
            hid,
            slope,
            hwt,
            *ones,
            *twos,
            *strips,
        )
        first, last = stage == order[0], stage == order[-1]
        dpre, small, *ends = call(
            functools.partial(
                middle_kernel, stage=stage, counts=(len(ones), len(twos)), ncol=ncol, first=first, last=last, nbins=nbins
            ),
            "middle",
            [shape(field), shape((channels, 128), F32)] + [shape(strip)] * (2 * last),
            args + (() if first else (dpre, small, taps)),
            us=5,
            smem=2,
            scratch=[
                pltpu.VMEM((nb * rows, 128), F32),
                pltpu.VMEM((channels, 128), F32),
                pltpu.VMEM((nb * 8, 128), F32),
                pltpu.VMEM((channels, 128), F32),
                pltpu.VMEM((8, 128), F32),
            ],
            aliases=None if first else {len(args): 0},
        )
        square = (wide, wide)
        pieces = shape((total // count, 128), F32)
        taps = call(
            functools.partial(weight_kernel, stage=stage, first=first),
            "weights",
            [pieces] * count if last else shape(square, F32),
            (scal, xs, dpre, small) + (() if first else (taps,)),
            us=2.5,
            mib=8,
            smem=1,
            scratch=[pltpu.VMEM(square, F32), pltpu.VMEM((total, 128), F32)] * last
            + [pltpu.VMEM((rows + 16, channels, 128), BF16)],
        )

    pieces = taps
    above, below = row_halo(*ends)
    sides = side_columns(dpre, above, below, scal)
    sides, pieces = lax.optimization_barrier((sides, pieces))
    ds = with_border(inner_of(dpre), above, below, sides, scal)
    parts = total_over_tiles(pieces)

    pair_gradient = pl.pallas_call(
        backward_kernel,
        grid=(rows // 8,),
        in_specs=[VM, VM],
        out_specs=pl.BlockSpec((channels, 8, width), lambda g: (0, g, 0)),
        out_shape=shape((channels, rows, width)),
        scratch_shapes=[pltpu.VMEM((tiles * channels * 8, 128), F32)],
        compiler_params=grant(8),
        cost_estimate=cost(6),
        name="backward",
    )(ds, w_bwd)

    conv_grad, biases, heads, head_biases, loss = pl.pallas_call(
        unpack_kernel,
        in_specs=[SM] + [VM] * len(parts),
        out_shape=[
            shape((3, 3, channels, channels), F32),
            shape((1, channels), F32),
            shape((nbins, channels), F32),
            shape((1, nbins), F32),
            shape((1, 1), F32),
        ],
        scratch_shapes=[pltpu.VMEM((total, 128), F32)],
        compiler_params=grant(4),
        cost_estimate=cost(1),
        name="unpack",
    )(scal, *parts)
    return (
        pair_gradient,
        conv_grad,
        biases.reshape(channels),
        heads,
        head_biases.reshape(nbins),
        loss.reshape(1),
    )


def solution(mesh):
    return jax.shard_map(
        per_device,
        mesh=mesh,
        in_specs=(
            P(None, ("parts", "row"), "col"),
            P(("parts", "row", "col"), None),
            P("parts"),
            P(),
            P(),
            P(),
            P(),
        ),
        out_specs=(
            P(None, ("parts", "row"), "col"),
            P("parts", None, None, None),
            P("parts"),
            P("parts", None),
            P("parts"),
            P("parts"),
        ),
        check_vma=False,
    )
```

```python
import functools

import jax
import jax.numpy as jnp
from jax import lax
from jax.experimental import pallas as pl
from jax.experimental.pallas import tpu as pltpu
from jax.sharding import PartitionSpec as P

DIL = 4
ROWS = ("row", "col")
F32 = jnp.float32
BF16 = jnp.bfloat16
VM = pl.BlockSpec(memory_space=pltpu.VMEM)
SM = pl.BlockSpec(memory_space=pltpu.SMEM)
MIB = 1024 * 1024


def grant(mib):
    return pltpu.CompilerParams(vmem_limit_bytes=mib * MIB)


def cost(us):
    return pl.CostEstimate(flops=int(us * 1.1e9), transcendentals=0, bytes_accessed=0)


def call(body, name, out_shape, args, us, smem=0, scratch=(), aliases=None, mib=12):
    return pl.pallas_call(
        body,
        out_shape=out_shape,
        in_specs=[SM] * smem + [VM] * (len(args) - smem),
        out_specs=jax.tree.map(lambda _: VM, out_shape),
        scratch_shapes=list(scratch),
        input_output_aliases=aliases or {},
        compiler_params=grant(mib),
        cost_estimate=cost(us),
        name=name,
    )(*args)


def shape(dims, dtype=BF16):
    return jax.ShapeDtypeStruct(dims, dtype)


def pairs_of(tiles):
    return jnp.concatenate(tiles, axis=1)


def prep_kernel(_, x, out, head, tail, landed, main, sems):
    channels, rows, width = x.shape
    tiles = width // 128
    some = channels // sems.shape[0]
    copies = [
        pltpu.make_async_copy(
            x.at[pl.ds(n * some, some)], landed.at[pl.ds(n * some, some)], sems.at[n]
        )
        for n in range(sems.shape[0])
    ]
    for copy in copies:
        copy.start()
    for n, copy in enumerate(copies):
        copy.wait()
        for c in range(n * some, (n + 1) * some):
            body = landed[c].astype(F32)
            for u in range(tiles):
                at = (u * channels + c) * (rows + 1)
                main[at : at + rows, :] = body[:, 128 * u : 128 * (u + 1)]

    def turn(i, _):
        for u in range(tiles):
            at = u * channels * (rows + 1) + i
            out[u, i] = main[pl.ds(at, channels, stride=rows + 1), :].astype(BF16)
        return 0

    lax.fori_loop(0, rows, turn, 0, unroll=8)
    for u in range(tiles):
        head[u] = out[u, :DIL]
        tail[u] = out[u, rows - DIL :]


def setup_kernel(scal, cw, cb, hw, labels, _, fwd, bwd, bias, head, headt, *pieces):
    ch = cw.shape[2]
    nbins, nb = hw.shape[0], head.shape[0]
    for a in range(3):
        for b in range(3):
            at = (3 * a + b) * ch
            fwd[:, at : at + ch] = cw[a, b]
            bwd[:, at : at + ch] = cw[2 - a, 2 - b].astype(F32).T.astype(BF16)
    bias[...] = jnp.broadcast_to(cb[...], (ch, ch)).T[:, 0:1]
    full = jnp.concatenate([hw[...].astype(F32), jnp.zeros((nb - nbins, ch), F32)], axis=0)
    head[...] = full.astype(BF16)
    headt[...] = full.T.astype(BF16)
    ncol, width = len(pieces), pieces[0].shape[1]
    blocks = [labels[:, width * n : width * (n + 1)] for n in range(ncol)]
    for d, piece in enumerate(pieces):
        want = lax.rem(scal[4] + d, ncol)
        value = blocks[0]
        for n in range(1, ncol):
            value = jnp.where(want == n, blocks[n], value)
        piece[...] = value.astype(F32).astype(BF16)


def edges_kernel(scal, field, above, below, *sides, ncol):
    tiles, rows, channels, _ = field.shape
    lane = lax.broadcasted_iota(jnp.int32, (channels, 128), 1) // DIL
    if ncol == 2:
        first = scal[4] == 0
        picks = [(jnp.where(first, tiles - 1, 0), jnp.where(first, DIL, 0))]
    else:
        picks = [(0, 0), (tiles - 1, DIL)]
    per = 128 // DIL
    for (tile, extra), out in zip(picks, sides):

        def add(slot, row, acc):
            turn = slot * DIL + extra
            turn = turn % 128 if isinstance(turn, int) else lax.rem(turn, 128)
            moved = pltpu.roll(row.astype(F32), turn, 1)
            return jnp.where(lane == slot, moved, acc)

        for part in range(out.shape[0]):
            acc = jnp.zeros((channels, 128), F32)
            start = part * per - DIL
            if part == 0:
                for ii in range(DIL):
                    acc = add(ii, above[tile, ii], acc)
                start = 0
            stop = min((part + 1) * per - DIL, rows)

            def body(i, acc):
                return add(i + DIL - part * per, field[tile, i], acc)

            for i in range(start, stop):
                acc = body(i, acc)
            if part == out.shape[0] - 1:
                for ii in range(DIL):
                    acc = add(rows + DIL + ii - part * per, below[tile, ii], acc)
            out[part] = acc.astype(BF16)


def place(out, i, row):
    tiles = len(row)
    lane = lax.broadcasted_iota(jnp.int32, row[0].shape, 1)
    whole = pairs_of([v.astype(F32) for v in row])
    before = pltpu.roll(whole, DIL, 1)
    after = pltpu.roll(whole, whole.shape[1] - DIL, 1)
    for u in range(tiles):
        b = before[:, 128 * u : 128 * (u + 1)]
        a = after[:, 128 * u : 128 * (u + 1)]
        if u == 0:
            b = jnp.where(lane < DIL, 0.0, b)
        if u == tiles - 1:
            a = jnp.where(lane >= 128 - DIL, 0.0, a)
        out[u, i] = jnp.concatenate([b.astype(BF16), row[u], a.astype(BF16)], axis=0)


def inner_kernel(field, out):
    tiles, rows = field.shape[:2]

    def body(i, _):
        place(out, i + DIL, [field[u, i] for u in range(tiles)])
        return 0

    lax.fori_loop(0, rows, body, 0, unroll=8)


def border_kernel(scal, above, below, *rest, ncol):
    sides, (_, out) = rest[:-2], rest[-2:]
    tiles, high, wide, _ = out.shape
    channels = wide // 3
    for i in range(DIL):
        place(out, i, [above[u, i] for u in range(tiles)])
        place(out, i + high - DIL, [below[u, i] for u in range(tiles)])
    lane = lax.broadcasted_iota(jnp.int32, (channels, 128), 1)
    per = 128 // DIL
    if ncol == 2:
        first = scal[4] == 0
        tile = jnp.where(first, tiles - 1, 0)
        block = pl.multiple_of(jnp.where(first, 2 * channels, 0), channels)
        base = jnp.where(first, 128 - DIL, 0)
        jobs = [(sides[0], tile, block, base)]
    else:
        jobs = [(sides[0], 0, 0, 0), (sides[1], tiles - 1, 2 * channels, 128 - DIL)]
    for side, tile, block, base in jobs:
        mine = (lane >= base) & (lane < base + DIL)
        for part in range(side.shape[0]):

            def patch(ii, _):
                i = part * per + ii
                moved = pltpu.roll(
                    side[part].astype(F32), lax.rem(128 + base - ii * DIL, 128), 1
                )
                spot = (tile, i, pl.ds(block, channels))
                out[spot] = jnp.where(mine, moved, out[spot].astype(F32)).astype(BF16)
                return 0

            lax.fori_loop(0, min(per, high - part * per), patch, 0, unroll=8)


def forward_kernel(scal, xs, w, bias, hw, hid, slope, direct, one, two, *, stage):
    rows, channels, _ = hid.shape
    nb = hw.shape[0]
    high = direct.shape[0] // nb
    rq = scal[0]
    u = (rq >> 1) ^ stage

    def window(i):
        return jnp.concatenate([xs[u, i + DIL * a] for a in range(3)], axis=0)

    def conv(g, _):
        for p in range(8):
            i = g * 64 + 8 * p
            pre = jnp.dot(
                w[...],
                pairs_of([window(i + e) for e in range(8)]),
                preferred_element_type=F32,
            )
            pre = pre + bias[...]
            grown = jnp.exp(jnp.minimum(pre, 0.0))
            h = jnp.where(pre > 0, pre, grown - 1.0).astype(BF16)
            s = jnp.where(pre > 0, 1.0, grown).astype(BF16)
            for e in range(8):
                hid[i + e] = h[:, 128 * e : 128 * (e + 1)]
                slope[i + e] = s[:, 128 * e : 128 * (e + 1)]
        return 0

    lax.fori_loop(0, rows // 64, conv, 0)

    def head(g, _):
        for p in range(8):
            i = g * 64 + 8 * p
            d = jnp.dot(hw[...], pairs_of([hid[i + e] for e in range(8)]), preferred_element_type=F32)
            for e in range(8):
                direct[pl.ds(i + e, nb, stride=high), :] = d[:, 128 * e : 128 * (e + 1)]
        return 0

    lax.fori_loop(0, rows // 64, head, 0)

    flip = (rq & 1) == 1
    for m in range(one.shape[0]):
        both = [direct[high * k : high * k + rows, :] for k in (2 * m, 2 * m + 1)]
        turned = jnp.concatenate(both, axis=0).T.astype(BF16)
        upper, lower = turned[:rows].astype(F32), turned[rows:].astype(F32)
        one[m] = jnp.where(flip, lower, upper).astype(BF16)
        two[m] = jnp.where(flip, upper, lower).astype(BF16)


def middle_kernel(scal, hb, direct, hid, slope, hwt, *rest, stage, counts, ncol, first, last, nbins):
    ones, twos, rest = rest[: counts[0]], rest[counts[0] : sum(counts)], rest[sum(counts) :]
    strips, rest = rest[:ncol], rest[ncol:]
    if not first:
        before, rest = rest[1], rest[3:]
    dpre, small, *ends, dl, hacc, bacc, cacc, lacc = rest
    nb, high, _ = direct.shape
    rows = hid.shape[0]
    band = rows // ncol
    channels = hwt.shape[0]
    rq, extent = scal[0], scal[3]
    u = (rq >> 1) ^ stage
    flip = (rq & 1) == 1
    crossed = scal[5] == 1
    for ref in (hacc, bacc, cacc, lacc):
        ref[...] = jnp.zeros_like(ref)
    dl[nbins * high :, :] = jnp.zeros((dl.shape[0] - nbins * high, 128), F32)

    lane = lax.broadcasted_iota(jnp.int32, (8, 128), 1)
    low = lane < 64
    col_ids = scal[2] + 128 * u + lane
    area = (extent * extent).astype(F32)

    def softmax(g, _):
        base = pl.multiple_of(g * 8, 8)
        row_ids = scal[1] + base + lax.broadcasted_iota(jnp.int32, (8, 128), 0)
        valid = jnp.where((row_ids < extent) & (col_ids < extent), 1.0, 0.0)
        strip, at = base // band, pl.multiple_of(lax.rem(base, band), 8)
        wanted = jnp.zeros((8, 128), F32)
        for d in range(ncol):
            here = lax.rem(scal[4] + ncol - strip, ncol) == d
            rows8 = strips[d][pl.ds(at, 8), :].astype(F32)
            for v in range(rows8.shape[1] // 128):
                lanes = rows8[:, 128 * v : 128 * (v + 1)]
                wanted = jnp.where(here & (u == v), lanes, wanted)
        logits = []
        for m in range((nbins + 1) // 2):
            a, b = (
                [ref[m, pl.ds(base, 8), :].astype(F32) for ref in refs] for refs in (ones, twos)
            )
            a = a[0] if len(a) == 1 else jnp.where(crossed, a[1], a[0])
            b = b[0] if len(b) == 1 else jnp.where(crossed, b[1], b[0])
            a, b = jnp.where(flip, b, a), jnp.where(flip, a, b)
            mirror = (
                jnp.where(low, a, pltpu.roll(b, 64, 1)),
                jnp.where(low, pltpu.roll(a, 64, 1), b),
            )
            for k in range(2 * m, min(2 * m + 2, nbins)):
                logits.append(
                    0.5 * (direct[k, pl.ds(base, 8), :] + mirror[k - 2 * m]) + hb[k]
                )
        peak = functools.reduce(jnp.maximum, logits)
        picked = functools.reduce(
            lambda a, b: a + b,
            [jnp.where(wanted == k, logits[k], 0.0) for k in range(nbins)],
        )
        powers = [jnp.exp(v - peak) for v in logits]
        total = functools.reduce(lambda a, b: a + b, powers)
        lacc[...] += valid * (peak + jnp.log(total) - picked)
        inverse = 1.0 / total
        scale = valid / area
        for k in range(nbins):
            d = (powers[k] * inverse - jnp.where(wanted == k, 1.0, 0.0)) * scale
            d = d.astype(BF16).astype(F32)
            dl[pl.ds(k * high + base, 8), :] = d
            bacc[8 * k : 8 * k + 8, :] += d
        return 0

    lax.fori_loop(0, rows // 8, softmax, 0, unroll=2)

    def back(g, _):
        heads, shifts = [], []
        for p in range(8):
            i = g * 64 + 8 * p
            d = pairs_of(
                [dl[pl.ds(i + e, nb, stride=high), :].astype(BF16) for e in range(8)]
            )
            h = pairs_of([hid[i + e] for e in range(8)])
            s = pairs_of([slope[i + e] for e in range(8)])
            v = jnp.dot(hwt[...], d, preferred_element_type=F32) * s.astype(F32)
            v = v.astype(BF16)
            for e in range(8):
                dpre[u, i + e] = v[:, 128 * e : 128 * (e + 1)]
                shifts.append(v[:, 128 * e : 128 * (e + 1)].astype(F32))
            heads.append((d, h))
        cacc[...] += functools.reduce(lambda a, b: a + b, shifts)
        hacc[0:nb, 0:channels] += lax.dot_general(
            pairs_of([d for d, _ in heads]), pairs_of([h for _, h in heads]),
            (((1,), (1,)), ((), ())), preferred_element_type=F32,
        )
        return 0

    lax.fori_loop(0, rows // 64, back, 0)

    spot = lax.broadcasted_iota(jnp.int32, small.shape, 1)
    sums = jnp.sum(bacc[...].reshape(nb, 8, 128), axis=1)
    sums = jnp.sum(sums, axis=1, keepdims=True)
    sums = jnp.concatenate([sums, jnp.zeros((channels - nb, 1), F32)], axis=0)
    biases = jnp.sum(cacc[...], axis=1, keepdims=True)
    loss = jnp.sum(jnp.sum(lacc[...], axis=1, keepdims=True), axis=0, keepdims=True)
    value = jnp.where(
        spot < channels,
        hacc[...],
        jnp.where(spot == channels, sums, jnp.where(spot == channels + 1, biases, loss)),
    )
    small[...] = value if first else value + before[...]
    if last:
        for v in range(dpre.shape[0]):
            ends[0][v] = dpre[v, :DIL]
            ends[1][v] = dpre[v, rows - DIL :]


def sum_kernel(*refs):
    refs[-1][...] = functools.reduce(lambda a, b: a + b, [ref[...] for ref in refs[:-1]])


def sum_of(values):
    return call(sum_kernel, "sum", shape(values[0].shape, F32), tuple(values), us=0.5, mib=2)


def weight_kernel(scal, xs, dpre, small, *rest, stage, first):
    if not first:
        before, rest = rest[0], rest[1:]
    padded, outs = rest[-1], rest[:-1]
    _, rows, channels, _ = dpre.shape
    wide = 3 * channels
    u = (scal[0] >> 1) ^ stage
    padded[0:8] = jnp.zeros((8, channels, 128), BF16)
    padded[8 : 8 + rows] = dpre[u]
    padded[8 + rows :] = jnp.zeros((8, channels, 128), BF16)

    def body(g, acc):
        left, right = [], []
        for ii in range(3 * 24):
            i = g * 72 + ii
            left.append(
                jnp.concatenate([padded[i + 8 - DIL * a] for a in range(3)], axis=0)
            )
            right.append(xs[u, i])
        acc[...] += lax.dot_general(
            pairs_of(left), pairs_of(right), (((1,), (1,)), ((), ())),
            preferred_element_type=F32,
        )

    acc = outs[-1] if len(outs) == 1 else outs[-2]
    acc[...] = jnp.zeros_like(acc) if first else before[...]
    lax.fori_loop(0, (rows + 8) // 72, lambda g, _: body(g, acc), None)
    if len(outs) == 1:
        return
    out, outs = outs[-1], outs[:-2]
    half = wide // 2
    out[0:wide, :] = acc[:, 0:128]
    out[wide : wide + half, 0:64] = acc[0:half, 128:192]
    out[wide : wide + half, 64:128] = acc[half:wide, 128:192]
    out[wide + half :, :] = small[...]
    for n, piece in enumerate(outs):
        size = piece.shape[0]
        piece[...] = out[pl.ds(pl.multiple_of((scal[6] ^ n) * size, 8), size), :]


def backward_kernel(ds, w, out, turned):
    step = pl.program_id(0)
    channels, some, width = out.shape
    tiles = width // 128
    for ii in range(some):
        i = step * some + ii
        window = pairs_of(
            [
                jnp.concatenate([ds[u, i + DIL * a] for a in range(3)], axis=0)
                for u in range(tiles)
            ]
        )
        v = jnp.dot(w[...], window, preferred_element_type=F32)
        for u in range(tiles):
            turned[pl.ds(u * channels * (some + 8) + ii, channels, stride=some + 8), :] = v[
                :, 128 * u : 128 * (u + 1)
            ]
    for u in range(tiles):
        at = (some + 8) * channels * u
        block = turned[at : at + (some + 8) * channels, :].reshape(channels, some + 8, 128)
        out[:, :, 128 * u : 128 * (u + 1)] = block[:, :some].astype(BF16)


def side_columns(field, above, below, scal):
    parts = -(-(field.shape[1] + 2 * DIL) * DIL // 128)
    ncol = lax.axis_size("col")
    return call(
        functools.partial(edges_kernel, ncol=ncol),
        "edges",
        [shape((parts, field.shape[2], 128))] * (1 if ncol == 2 else 2),
        (scal, field, above, below),
        us=1.5,
        smem=1,
    )


def with_border(inner, above, below, sides, scal):
    ncol = lax.axis_size("col")
    if ncol == 2:
        got = [lax.ppermute(sides[0], "col", [(0, 1), (1, 0)])]
    else:
        to_left, to_right = sides
        got = [
            lax.ppermute(to_right, "col", [(i, i + 1) for i in range(ncol - 1)]),
            lax.ppermute(to_left, "col", [(i + 1, i) for i in range(ncol - 1)]),
        ]
    return call(
        functools.partial(border_kernel, ncol=ncol),
        "border",
        shape(inner.shape),
        (scal, above, below, *got, inner),
        us=1.5,
        smem=1,
        aliases={3 + len(got): 0},
    )


def inner_of(field):
    tiles, rows, channels, _ = field.shape
    return call(
        inner_kernel,
        "inner",
        shape((tiles, rows + 2 * DIL, 3 * channels, 128)),
        (field,),
        us=3,
    )


def row_halo(head, tail):
    count = lax.axis_size("row")
    above = lax.ppermute(tail, "row", [(i, i + 1) for i in range(count - 1)])
    below = lax.ppermute(head, "row", [(i + 1, i) for i in range(count - 1)])
    return above, below


def piece_count(total):
    nrow, ncol = lax.axis_size("row"), lax.axis_size("col")
    return 4 if ncol == 2 and nrow % 2 == 0 and nrow <= 8 and total % 32 == 0 else 1


def total_over_tiles(pieces):
    nrow, ncol = lax.axis_size("row"), lax.axis_size("col")
    if len(pieces) == 4:
        def near(v, d):
            perm = [
                (i * 2 + j, (i ^ (d >> 1)) * 2 + (j ^ (d & 1)))
                for i in range(nrow)
                for j in range(2)
            ]
            return lax.ppermute(v, ROWS, perm)

        own = sum_of([pieces[0]] + [near(pieces[d], d) for d in (1, 2, 3)])
        turns = [[(i, (i + 2 * d) % nrow) for i in range(nrow)] for d in range(1, nrow // 2)]
        own = sum_of([own] + [lax.ppermute(own, "row", turn) for turn in turns])
        return [own] + [near(own, d) for d in (1, 2, 3)]
    value = pieces[0]
    for axis, count in (("col", ncol), ("row", nrow)):
        if count & (count - 1):
            value = lax.psum(value, axis)
            continue
        bit = 1
        while bit < count:
            value = value + lax.ppermute(value, axis, [(i, i ^ bit) for i in range(count)])
            bit *= 2
    return [value]


def unpack_kernel(scal, *rest):
    parts, (taps, biases, heads, head_biases, loss, buf) = rest[:-6], rest[-6:]
    for n, part in enumerate(parts):
        size = part.shape[0]
        buf[pl.ds(pl.multiple_of((scal[6] ^ n) * size, 8), size), :] = part[...]
    ch = taps.shape[2]
    half = 3 * ch // 2
    for a in range(3):
        taps[a, 0] = buf[a * ch : (a + 1) * ch, 0:ch]
        taps[a, 1] = buf[a * ch : (a + 1) * ch, ch : 2 * ch]
        for o in range(0, ch, 32):
            at = a * ch + o
            lanes = slice(0, ch) if at < half else slice(ch, 2 * ch)
            row = 3 * ch + at % half
            taps[a, 2, o : o + 32] = buf[row : row + 32, lanes]
    small = buf[3 * ch + half :, :]
    turned = small.T
    heads[...] = small[: heads.shape[0], :ch]
    head_biases[...] = turned[ch : ch + 1, : heads.shape[0]]
    biases[...] = turned[ch + 1 : ch + 2, :]
    area = (scal[3] * scal[3]).astype(F32)
    loss[...] = turned[ch + 2 : ch + 3, 0:1] / area


def per_device(x, labels, lengths, conv_weight, conv_bias, head_weight, head_bias):
    channels, rows, width = x.shape
    nbins = head_weight.shape[0]
    nrow, ncol = lax.axis_size("row"), lax.axis_size("col")
    q = width // rows
    tiles = width // 128
    assert rows == 64 and channels == 64 and q == 2 * tiles and q & (q - 1) == 0
    assert q * ncol == nrow and 128 * tiles == width
    nb = -(-nbins // 8) * 8
    pairs = (nbins + 1) // 2
    wide = 3 * channels
    total = wide + wide // 2 + channels
    r, c = lax.axis_index("row"), lax.axis_index("col")

    count = piece_count(total)
    mine = (r % 2) * 2 + c if count == 4 else 0 * r
    crossed = (r // q != c).astype(jnp.int32)
    scal = jnp.stack([r % q, r * rows, c * width, lengths[0], c, crossed, mine]).astype(jnp.int32)
    field = (tiles, rows, channels, 128)
    strip = (tiles, DIL, channels, 128)
    xt, head, tail = pl.pallas_call(
        prep_kernel,
        in_specs=[SM, pl.BlockSpec(memory_space=pltpu.HBM)],
        out_specs=[VM, VM, VM],
        out_shape=[shape(field), shape(strip), shape(strip)],
        scratch_shapes=[
            pltpu.VMEM(x.shape, BF16),
            pltpu.VMEM((tiles * channels * (rows + 1), 128), F32),
            pltpu.SemaphoreType.DMA((8,)),
        ],
        compiler_params=grant(8),
        cost_estimate=cost(4),
        name="prep",
    )(scal, pltpu.with_memory_space_constraint(x, pltpu.HBM))
    above, below = row_halo(head, tail)
    sides = side_columns(xt, above, below, scal)
    w_fwd, w_bwd, bias, hw, hwt, *mine = call(
        setup_kernel,
        "setup",
        [shape((channels, 9 * channels))] * 2
        + [shape((channels, 1), F32), shape((nb, channels)), shape((channels, nb))]
        + [shape((labels.shape[0], width))] * ncol,
        (scal, conv_weight, conv_bias[None], head_weight, labels, tail),
        us=2,
        smem=1,
    )
    strips = mine[:1] + [
        lax.ppermute(mine[d], "col", [(i, (i + d) % ncol) for i in range(ncol)])
        for d in range(1, ncol)
    ]
    xs = with_border(inner_of(xt), above, below, sides, scal)

    kept, got = [], []
    for stage in range(tiles):
        block = shape((pairs, rows, 128))
        hid, slope, direct, *sends = call(
            functools.partial(forward_kernel, stage=stage),
            "forward",
            [shape(field[1:]), shape(field[1:]), shape((nb * (rows + 8), 128), F32), block, block],
            (scal, xs, w_fwd, bias, hw),
            us=6,
            smem=1,
        )
        kept.append((hid, slope, direct))
        for e in range(2):
            t = 2 * stage + e
            perm = [
                (i * ncol + j, (q * j + (i % q ^ t)) * ncol + i // q)
                for i in range(nrow)
                for j in range(ncol)
            ]
            if ncol > 2 or e == 0:
                got.append([lax.ppermute(sends[e], ROWS, perm)])
                continue
            near = [(a, b) for a, b in perm if a % ncol == b % ncol]
            far = [(a, b) for a, b in perm if a % ncol != b % ncol]
            over = [(a, a + b % ncol - a % ncol) for a, b in far]
            along = [(a + b % ncol - a % ncol, b) for a, b in far]
            same = lax.ppermute(sends[e], ROWS, near)
            relayed = lax.ppermute(sends[e], ROWS, over)
            got.append([same, lax.ppermute(relayed, ROWS, along)])

    dpre = small = ends = taps = None
    order = list(range(tiles))
    for stage in order:
        hid, slope, direct = kept[stage]
        ones, twos = got[2 * stage : 2 * stage + 2]
        args = (
            scal,
            head_bias,
            direct.reshape(nb, rows + 8, 128),
            hid,
            slope,
            hwt,
            *ones,
            *twos,
            *strips,
        )
        first, last = stage == order[0], stage == order[-1]
        dpre, small, *ends = call(
            functools.partial(
                middle_kernel, stage=stage, counts=(len(ones), len(twos)), ncol=ncol, first=first, last=last, nbins=nbins
            ),
            "middle",
            [shape(field), shape((channels, 128), F32)] + [shape(strip)] * (2 * last),
            args + (() if first else (dpre, small, taps)),
            us=5,
            smem=2,
            scratch=[
                pltpu.VMEM((nb * (rows + 8), 128), F32),
                pltpu.VMEM((channels, 128), F32),
                pltpu.VMEM((nb * 8, 128), F32),
                pltpu.VMEM((channels, 128), F32),
                pltpu.VMEM((8, 128), F32),
            ],
            aliases=None if first else {len(args): 0},
        )
        square = (wide, wide)
        pieces = shape((total // count, 128), F32)
        taps = call(
            functools.partial(weight_kernel, stage=stage, first=first),
            "weights",
            [pieces] * count if last else shape(square, F32),
            (scal, xs, dpre, small) + (() if first else (taps,)),
            us=2.5,
            mib=12,
            smem=1,
            scratch=[pltpu.VMEM(square, F32), pltpu.VMEM((total, 128), F32)] * last
            + [pltpu.VMEM((rows + 16, channels, 128), BF16)],
        )

    pieces = taps
    above, below = row_halo(*ends)
    sides = side_columns(dpre, above, below, scal)
    sides, pieces = lax.optimization_barrier((sides, pieces))
    ds = with_border(inner_of(dpre), above, below, sides, scal)
    parts = total_over_tiles(pieces)

    pair_gradient = pl.pallas_call(
        backward_kernel,
        grid=(rows // 16,),
        in_specs=[VM, VM],
        out_specs=pl.BlockSpec((channels, 16, width), lambda g: (0, g, 0)),
        out_shape=shape((channels, rows, width)),
        scratch_shapes=[pltpu.VMEM((tiles * channels * 24, 128), F32)],
        compiler_params=grant(8),
        cost_estimate=cost(6),
        name="backward",
    )(ds, w_bwd)

    conv_grad, biases, heads, head_biases, loss = pl.pallas_call(
        unpack_kernel,
        in_specs=[SM] + [VM] * len(parts),
        out_shape=[
            shape((3, 3, channels, channels), F32),
            shape((1, channels), F32),
            shape((nbins, channels), F32),
            shape((1, nbins), F32),
            shape((1, 1), F32),
        ],
        scratch_shapes=[pltpu.VMEM((total, 128), F32)],
        compiler_params=grant(4),
        cost_estimate=cost(1),
        name="unpack",
    )(scal, *parts)
    return (
        pair_gradient,
        conv_grad,
        biases.reshape(channels),
        heads,
        head_biases.reshape(nbins),
        loss.reshape(1),
    )


def solution(mesh):
    return jax.shard_map(
        per_device,
        mesh=mesh,
        in_specs=(
            P(None, ("parts", "row"), "col"),
            P(("parts", "row", "col"), None),
            P("parts"),
            P(),
            P(),
            P(),
            P(),
        ),
        out_specs=(
            P(None, ("parts", "row"), "col"),
            P("parts", None, None, None),
            P("parts"),
            P("parts", None),
            P("parts"),
            P("parts"),
        ),
        check_vma=False,
    )
```

```python
import functools

import jax
import jax.numpy as jnp
from jax import lax
from jax.experimental import pallas as pl
from jax.experimental.pallas import tpu as pltpu
from jax.sharding import PartitionSpec as P

DIL = 4
ROWS = ("row", "col")
F32 = jnp.float32
BF16 = jnp.bfloat16
VM = pl.BlockSpec(memory_space=pltpu.VMEM)
SM = pl.BlockSpec(memory_space=pltpu.SMEM)
MIB = 1024 * 1024


def grant(mib):
    return pltpu.CompilerParams(vmem_limit_bytes=mib * MIB)


def cost(us):
    return pl.CostEstimate(flops=int(us * 1.1e9), transcendentals=0, bytes_accessed=0)


def call(body, name, out_shape, args, us, smem=0, scratch=(), aliases=None, mib=12):
    return pl.pallas_call(
        body,
        out_shape=out_shape,
        in_specs=[SM] * smem + [VM] * (len(args) - smem),
        out_specs=jax.tree.map(lambda _: VM, out_shape),
        scratch_shapes=list(scratch),
        input_output_aliases=aliases or {},
        compiler_params=grant(mib),
        cost_estimate=cost(us),
        name=name,
    )(*args)


def shape(dims, dtype=BF16):
    return jax.ShapeDtypeStruct(dims, dtype)


def pairs_of(tiles):
    return jnp.concatenate(tiles, axis=1)


def prep_kernel(_, x, out, head, tail, landed, main, sems):
    channels, rows, width = x.shape
    tiles = width // 128
    some = channels // sems.shape[0]
    copies = [
        pltpu.make_async_copy(
            x.at[pl.ds(n * some, some)], landed.at[pl.ds(n * some, some)], sems.at[n]
        )
        for n in range(sems.shape[0])
    ]
    for copy in copies:
        copy.start()
    for n, copy in enumerate(copies):
        copy.wait()
        for c in range(n * some, (n + 1) * some):
            body = landed[c].astype(F32)
            for u in range(tiles):
                at = (u * channels + c) * (rows + 1)
                main[at : at + rows, :] = body[:, 128 * u : 128 * (u + 1)]

    def turn(i, _):
        for u in range(tiles):
            at = u * channels * (rows + 1) + i
            out[u, i] = main[pl.ds(at, channels, stride=rows + 1), :].astype(BF16)
        return 0

    lax.fori_loop(0, rows, turn, 0, unroll=8)
    for u in range(tiles):
        head[u] = out[u, :DIL]
        tail[u] = out[u, rows - DIL :]


def setup_kernel(scal, cw, cb, hw, labels, _, fwd, bwd, bias, head, headt, *pieces):
    ch = cw.shape[2]
    nbins, nb = hw.shape[0], head.shape[0]
    for a in range(3):
        for b in range(3):
            at = (3 * a + b) * ch
            fwd[:, at : at + ch] = cw[a, b]
            bwd[:, at : at + ch] = cw[2 - a, 2 - b].astype(F32).T.astype(BF16)
    bias[...] = jnp.broadcast_to(cb[...], (ch, ch)).T[:, 0:1]
    full = jnp.concatenate([hw[...].astype(F32), jnp.zeros((nb - nbins, ch), F32)], axis=0)
    head[...] = full.astype(BF16)
    headt[...] = full.T.astype(BF16)
    ncol = len(pieces)
    band, width = labels.shape[0], labels.shape[1] // ncol
    blocks = [labels[:, width * n : width * (n + 1)] for n in range(ncol)]
    for d, piece in enumerate(pieces):
        want = lax.rem(scal[4] + d, ncol)
        value = blocks[0]
        for n in range(1, ncol):
            value = jnp.where(want == n, blocks[n], value)
        value = value.astype(F32).astype(BF16)
        for u in range(width // 128):
            piece[band * u : band * (u + 1), :] = value[:, 128 * u : 128 * (u + 1)]


def edges_kernel(scal, field, above, below, *sides, ncol, extra):
    tiles, rows, channels, _ = field.shape
    lane = lax.broadcasted_iota(jnp.int32, (channels, 128), 1) // DIL
    if ncol == 2:
        first = scal[4] == 0
        picks = [(jnp.where(first, tiles - 1, 0), jnp.where(first, DIL, 0))]
    else:
        picks = [(0, 0), (tiles - 1, DIL)]
    per = 128 // DIL
    if extra:
        sides[1][sides[1].shape[0] - 1] = sides[0][...]
        sides = sides[1:]
    for (tile, offset), out in zip(picks, sides):

        def add(slot, row, acc):
            turn = slot * DIL + offset
            turn = turn % 128 if isinstance(turn, int) else lax.rem(turn, 128)
            moved = pltpu.roll(row.astype(F32), turn, 1)
            return jnp.where(lane == slot, moved, acc)

        parts = out.shape[0] - extra
        for part in range(parts):
            acc = jnp.zeros((channels, 128), F32)
            start = part * per - DIL
            if part == 0:
                for ii in range(DIL):
                    acc = add(ii, above[tile, ii], acc)
                start = 0
            stop = min((part + 1) * per - DIL, rows)

            def body(i, acc):
                return add(i + DIL - part * per, field[tile, i], acc)

            for i in range(start, stop):
                acc = body(i, acc)
            if part == parts - 1:
                for ii in range(DIL):
                    acc = add(rows + DIL + ii - part * per, below[tile, ii], acc)
            out[part] = acc.astype(BF16)


def place(out, i, row):
    tiles = len(row)
    lane = lax.broadcasted_iota(jnp.int32, row[0].shape, 1)
    whole = pairs_of([v.astype(F32) for v in row])
    before = pltpu.roll(whole, DIL, 1)
    after = pltpu.roll(whole, whole.shape[1] - DIL, 1)
    for u in range(tiles):
        b = before[:, 128 * u : 128 * (u + 1)]
        a = after[:, 128 * u : 128 * (u + 1)]
        if u == 0:
            b = jnp.where(lane < DIL, 0.0, b)
        if u == tiles - 1:
            a = jnp.where(lane >= 128 - DIL, 0.0, a)
        out[u, i] = jnp.concatenate([b.astype(BF16), row[u], a.astype(BF16)], axis=0)


def inner_kernel(field, out):
    tiles, rows = field.shape[:2]

    def body(i, _):
        place(out, i + DIL, [field[u, i] for u in range(tiles)])
        return 0

    lax.fori_loop(0, rows, body, 0, unroll=8)


def border_kernel(scal, above, below, *rest, ncol):
    sides, (_, out) = rest[:-2], rest[-2:]
    tiles, high, wide, _ = out.shape
    channels = wide // 3
    for i in range(DIL):
        place(out, i, [above[u, i] for u in range(tiles)])
        place(out, i + high - DIL, [below[u, i] for u in range(tiles)])
    lane = lax.broadcasted_iota(jnp.int32, (channels, 128), 1)
    per = 128 // DIL
    if ncol == 2:
        first = scal[4] == 0
        tile = jnp.where(first, tiles - 1, 0)
        block = pl.multiple_of(jnp.where(first, 2 * channels, 0), channels)
        base = jnp.where(first, 128 - DIL, 0)
        jobs = [(sides[0], tile, block, base)]
    else:
        jobs = [(sides[0], 0, 0, 0), (sides[1], tiles - 1, 2 * channels, 128 - DIL)]
    for side, tile, block, base in jobs:
        mine = (lane >= base) & (lane < base + DIL)
        for part in range(-(-high // per)):

            def patch(ii, _):
                i = part * per + ii
                moved = pltpu.roll(
                    side[part].astype(F32), lax.rem(128 + base - ii * DIL, 128), 1
                )
                spot = (tile, i, pl.ds(block, channels))
                out[spot] = jnp.where(mine, moved, out[spot].astype(F32)).astype(BF16)
                return 0

            lax.fori_loop(0, min(per, high - part * per), patch, 0, unroll=8)


def forward_kernel(scal, xs, w, bias, hw, hid, slope, direct, one, two, *, stage, swap):
    rows, channels, _ = hid.shape
    nb = hw.shape[0]
    high = direct.shape[0] // nb
    rq = scal[0]
    u = (rq >> 1) ^ stage

    def window(i):
        return jnp.concatenate([xs[u, i + DIL * a] for a in range(3)], axis=0)

    def conv(g, _):
        for p in range(8):
            i = g * 64 + 8 * p
            pre = jnp.dot(
                w[...],
                pairs_of([window(i + e) for e in range(8)]),
                preferred_element_type=F32,
            )
            pre = pre + bias[...]
            grown = jnp.exp(jnp.minimum(pre, 0.0))
            h = jnp.where(pre > 0, pre, grown - 1.0).astype(BF16)
            s = jnp.where(pre > 0, 1.0, grown).astype(BF16)
            for e in range(8):
                hid[i + e] = h[:, 128 * e : 128 * (e + 1)]
                slope[i + e] = s[:, 128 * e : 128 * (e + 1)]
        return 0

    lax.fori_loop(0, rows // 64, conv, 0)

    def head(g, _):
        for p in range(8):
            i = g * 64 + 8 * p
            d = jnp.dot(hw[...], pairs_of([hid[i + e] for e in range(8)]), preferred_element_type=F32)
            for e in range(8):
                direct[pl.ds(i + e, nb, stride=high), :] = d[:, 128 * e : 128 * (e + 1)]
        return 0

    lax.fori_loop(0, rows // 64, head, 0)

    flip = ((rq & 1) ^ (1 - scal[5] if swap else 0)) == 1
    for m in range(one.shape[0]):
        both = [direct[high * k : high * k + rows, :] for k in (2 * m, 2 * m + 1)]
        turned = jnp.concatenate(both, axis=0).T.astype(BF16)
        upper, lower = turned[:rows].astype(F32), turned[rows:].astype(F32)
        one[m] = jnp.where(flip, lower, upper).astype(BF16)
        two[m] = jnp.where(flip, upper, lower).astype(BF16)


def middle_kernel(scal, hb, direct, hid, slope, hwt, *rest, stage, counts, ncol, first, last, nbins):
    ones, twos, rest = rest[: counts[0]], rest[counts[0] : sum(counts)], rest[sum(counts) :]
    strips, rest = rest[:ncol], rest[ncol:]
    if not first:
        before, rest = rest[1], rest[3:]
    dpre, small, *ends, dl, hacc, bacc, cacc, lacc = rest
    nb, high, _ = direct.shape
    rows = hid.shape[0]
    band = rows // ncol
    channels = hwt.shape[0]
    rq, extent = scal[0], scal[3]
    u = (rq >> 1) ^ stage
    flip = (rq & 1) == 1
    crossed = scal[5] == 1
    for ref in (hacc, bacc, cacc, lacc):
        ref[...] = jnp.zeros_like(ref)
    dl[nbins * high :, :] = jnp.zeros((dl.shape[0] - nbins * high, 128), F32)

    lane = lax.broadcasted_iota(jnp.int32, (8, 128), 1)
    low = lane < 64
    col_ids = scal[2] + 128 * u + lane
    area = (extent * extent).astype(F32)

    def softmax(g, _):
        base = pl.multiple_of(g * 8, 8)
        row_ids = scal[1] + base + lax.broadcasted_iota(jnp.int32, (8, 128), 0)
        valid = jnp.where((row_ids < extent) & (col_ids < extent), 1.0, 0.0)
        strip, at = base // band, pl.multiple_of(lax.rem(base, band), 8)
        wanted = jnp.zeros((8, 128), F32)
        for d in range(ncol):
            here = lax.rem(scal[4] + ncol - strip, ncol) == d
            rows8 = pl.ds(pl.multiple_of(u * band + at, 8), 8)
            if len(strips[d].shape) == 3:
                value = strips[d][strips[d].shape[0] - 1, rows8, :]
            else:
                value = strips[d][rows8, :]
            wanted = jnp.where(here, value.astype(F32), wanted)
        logits = []
        for m in range((nbins + 1) // 2):
            a, b = (
                [ref[m, pl.ds(base, 8), :].astype(F32) for ref in refs] for refs in (ones, twos)
            )
            a = a[0] if len(a) == 1 else jnp.where(crossed, a[1], a[0])
            b = b[0] if len(b) == 1 else jnp.where(crossed, b[1], b[0])
            a, b = jnp.where(flip, b, a), jnp.where(flip, a, b)
            mirror = (
                jnp.where(low, a, pltpu.roll(b, 64, 1)),
                jnp.where(low, pltpu.roll(a, 64, 1), b),
            )
            for k in range(2 * m, min(2 * m + 2, nbins)):
                logits.append(
                    0.5 * (direct[k, pl.ds(base, 8), :] + mirror[k - 2 * m]) + hb[k]
                )
        peak = functools.reduce(jnp.maximum, logits)
        picked = functools.reduce(
            lambda a, b: a + b,
            [jnp.where(wanted == k, logits[k], 0.0) for k in range(nbins)],
        )
        powers = [jnp.exp(v - peak) for v in logits]
        total = functools.reduce(lambda a, b: a + b, powers)
        lacc[...] += valid * (peak + jnp.log(total) - picked)
        inverse = 1.0 / total
        scale = valid / area
        for k in range(nbins):
            d = (powers[k] * inverse - jnp.where(wanted == k, 1.0, 0.0)) * scale
            d = d.astype(BF16).astype(F32)
            dl[pl.ds(k * high + base, 8), :] = d
            bacc[8 * k : 8 * k + 8, :] += d
        return 0

    lax.fori_loop(0, rows // 8, softmax, 0, unroll=2)

    def back(g, _):
        heads, shifts = [], []
        for p in range(8):
            i = g * 64 + 8 * p
            d = pairs_of(
                [dl[pl.ds(i + e, nb, stride=high), :].astype(BF16) for e in range(8)]
            )
            h = pairs_of([hid[i + e] for e in range(8)])
            s = pairs_of([slope[i + e] for e in range(8)])
            v = jnp.dot(hwt[...], d, preferred_element_type=F32) * s.astype(F32)
            v = v.astype(BF16)
            for e in range(8):
                dpre[u, i + e] = v[:, 128 * e : 128 * (e + 1)]
                shifts.append(v[:, 128 * e : 128 * (e + 1)].astype(F32))
            heads.append((d, h))
        cacc[...] += functools.reduce(lambda a, b: a + b, shifts)
        hacc[0:nb, 0:channels] += lax.dot_general(
            pairs_of([d for d, _ in heads]), pairs_of([h for _, h in heads]),
            (((1,), (1,)), ((), ())), preferred_element_type=F32,
        )
        return 0

    lax.fori_loop(0, rows // 64, back, 0)

    spot = lax.broadcasted_iota(jnp.int32, small.shape, 1)
    sums = jnp.sum(bacc[...].reshape(nb, 8, 128), axis=1)
    sums = jnp.sum(sums, axis=1, keepdims=True)
    sums = jnp.concatenate([sums, jnp.zeros((channels - nb, 1), F32)], axis=0)
    biases = jnp.sum(cacc[...], axis=1, keepdims=True)
    loss = jnp.sum(jnp.sum(lacc[...], axis=1, keepdims=True), axis=0, keepdims=True)
    value = jnp.where(
        spot < channels,
        hacc[...],
        jnp.where(spot == channels, sums, jnp.where(spot == channels + 1, biases, loss)),
    )
    small[...] = value if first else value + before[...]
    if last:
        for v in range(dpre.shape[0]):
            ends[0][v] = dpre[v, :DIL]
            ends[1][v] = dpre[v, rows - DIL :]


def sum_kernel(*refs):
    refs[-1][...] = functools.reduce(lambda a, b: a + b, [ref[...] for ref in refs[:-1]])


def sum_of(values):
    return call(sum_kernel, "sum", shape(values[0].shape, F32), tuple(values), us=0.5, mib=2)


def weight_kernel(scal, xs, dpre, small, *rest, stage, first):
    if not first:
        before, rest = rest[0], rest[1:]
    padded, outs = rest[-1], rest[:-1]
    _, rows, channels, _ = dpre.shape
    wide = 3 * channels
    u = (scal[0] >> 1) ^ stage
    padded[0:8] = jnp.zeros((8, channels, 128), BF16)
    padded[8 : 8 + rows] = dpre[u]
    padded[8 + rows :] = jnp.zeros((8, channels, 128), BF16)

    def body(g, acc):
        left, right = [], []
        for ii in range(3 * 24):
            i = g * 72 + ii
            left.append(
                jnp.concatenate([padded[i + 8 - DIL * a] for a in range(3)], axis=0)
            )
            right.append(xs[u, i])
        acc[...] += lax.dot_general(
            pairs_of(left), pairs_of(right), (((1,), (1,)), ((), ())),
            preferred_element_type=F32,
        )

    acc = outs[-1] if len(outs) == 1 else outs[-2]
    acc[...] = jnp.zeros_like(acc) if first else before[...]
    lax.fori_loop(0, (rows + 8) // 72, lambda g, _: body(g, acc), None)
    if len(outs) == 1:
        return
    out, outs = outs[-1], outs[:-2]
    half = wide // 2
    out[0:wide, :] = acc[:, 0:128]
    out[wide : wide + half, 0:64] = acc[0:half, 128:192]
    out[wide : wide + half, 64:128] = acc[half:wide, 128:192]
    out[wide + half :, :] = small[...]
    for n, piece in enumerate(outs):
        size = piece.shape[0]
        piece[...] = out[pl.ds(pl.multiple_of((scal[6] ^ n) * size, 8), size), :]


def backward_kernel(ds, w, out, turned):
    step = pl.program_id(0)
    channels, some, width = out.shape
    tiles = width // 128
    for ii in range(some):
        i = step * some + ii
        window = pairs_of(
            [
                jnp.concatenate([ds[u, i + DIL * a] for a in range(3)], axis=0)
                for u in range(tiles)
            ]
        )
        v = jnp.dot(w[...], window, preferred_element_type=F32)
        for u in range(tiles):
            turned[pl.ds(u * channels * (some + 8) + ii, channels, stride=some + 8), :] = v[
                :, 128 * u : 128 * (u + 1)
            ]
    for u in range(tiles):
        at = (some + 8) * channels * u
        block = turned[at : at + (some + 8) * channels, :].reshape(channels, some + 8, 128)
        out[:, :, 128 * u : 128 * (u + 1)] = block[:, :some].astype(BF16)


def side_columns(field, above, below, scal, more=()):
    parts = -(-(field.shape[1] + 2 * DIL) * DIL // 128)
    ncol = lax.axis_size("col")
    return call(
        functools.partial(edges_kernel, ncol=ncol, extra=len(more)),
        "edges",
        [shape((parts + len(more), field.shape[2], 128))] * (1 if ncol == 2 else 2),
        (scal, field, above, below, *more),
        us=1.5,
        smem=1,
    )


def with_border(inner, above, below, sides, scal):
    ncol = lax.axis_size("col")
    if ncol == 2:
        got = [lax.ppermute(sides[0], "col", [(0, 1), (1, 0)])]
    else:
        to_left, to_right = sides
        got = [
            lax.ppermute(to_right, "col", [(i, i + 1) for i in range(ncol - 1)]),
            lax.ppermute(to_left, "col", [(i + 1, i) for i in range(ncol - 1)]),
        ]
    return got, call(
        functools.partial(border_kernel, ncol=ncol),
        "border",
        shape(inner.shape),
        (scal, above, below, *got, inner),
        us=1.5,
        smem=1,
        aliases={3 + len(got): 0},
    )


def inner_of(field):
    tiles, rows, channels, _ = field.shape
    return call(
        inner_kernel,
        "inner",
        shape((tiles, rows + 2 * DIL, 3 * channels, 128)),
        (field,),
        us=3,
    )


def row_halo(head, tail):
    count = lax.axis_size("row")
    above = lax.ppermute(tail, "row", [(i, i + 1) for i in range(count - 1)])
    below = lax.ppermute(head, "row", [(i + 1, i) for i in range(count - 1)])
    return above, below


def piece_count(total):
    nrow, ncol = lax.axis_size("row"), lax.axis_size("col")
    return 4 if ncol == 2 and nrow % 2 == 0 and nrow <= 8 and total % 32 == 0 else 1


def total_over_tiles(pieces):
    nrow, ncol = lax.axis_size("row"), lax.axis_size("col")
    if len(pieces) == 4:
        def near(v, d):
            perm = [
                (i * 2 + j, (i ^ (d >> 1)) * 2 + (j ^ (d & 1)))
                for i in range(nrow)
                for j in range(2)
            ]
            return lax.ppermute(v, ROWS, perm)

        own = sum_of([pieces[0]] + [near(pieces[d], d) for d in (1, 2, 3)])
        turns = [[(i, (i + 2 * d) % nrow) for i in range(nrow)] for d in range(1, nrow // 2)]
        own = sum_of([own] + [lax.ppermute(own, "row", turn) for turn in turns])
        return [own] + [near(own, d) for d in (1, 2, 3)]
    value = pieces[0]
    for axis, count in (("col", ncol), ("row", nrow)):
        if count & (count - 1):
            value = lax.psum(value, axis)
            continue
        bit = 1
        while bit < count:
            value = value + lax.ppermute(value, axis, [(i, i ^ bit) for i in range(count)])
            bit *= 2
    return [value]


def unpack_kernel(scal, *rest):
    parts, (taps, biases, heads, head_biases, loss, buf) = rest[:-6], rest[-6:]
    for n, part in enumerate(parts):
        size = part.shape[0]
        buf[pl.ds(pl.multiple_of((scal[6] ^ n) * size, 8), size), :] = part[...]
    ch = taps.shape[2]
    half = 3 * ch // 2
    for a in range(3):
        taps[a, 0] = buf[a * ch : (a + 1) * ch, 0:ch]
        taps[a, 1] = buf[a * ch : (a + 1) * ch, ch : 2 * ch]
        for o in range(0, ch, 32):
            at = a * ch + o
            lanes = slice(0, ch) if at < half else slice(ch, 2 * ch)
            row = 3 * ch + at % half
            taps[a, 2, o : o + 32] = buf[row : row + 32, lanes]
    small = buf[3 * ch + half :, :]
    turned = small.T
    heads[...] = small[: heads.shape[0], :ch]
    head_biases[...] = turned[ch : ch + 1, : heads.shape[0]]
    biases[...] = turned[ch + 1 : ch + 2, :]
    area = (scal[3] * scal[3]).astype(F32)
    loss[...] = turned[ch + 2 : ch + 3, 0:1] / area


def per_device(x, labels, lengths, conv_weight, conv_bias, head_weight, head_bias):
    channels, rows, width = x.shape
    nbins = head_weight.shape[0]
    nrow, ncol = lax.axis_size("row"), lax.axis_size("col")
    q = width // rows
    tiles = width // 128
    assert rows == 64 and channels == 64 and q == 2 * tiles and q & (q - 1) == 0
    assert q * ncol == nrow and 128 * tiles == width
    nb = -(-nbins // 8) * 8
    pairs = (nbins + 1) // 2
    wide = 3 * channels
    total = wide + wide // 2 + channels
    r, c = lax.axis_index("row"), lax.axis_index("col")

    count = piece_count(total)
    mine = (r % 2) * 2 + c if count == 4 else 0 * r
    crossed = (r // q != c).astype(jnp.int32)
    scal = jnp.stack([r % q, r * rows, c * width, lengths[0], c, crossed, mine]).astype(jnp.int32)
    field = (tiles, rows, channels, 128)
    strip = (tiles, DIL, channels, 128)
    xt, head, tail = pl.pallas_call(
        prep_kernel,
        in_specs=[SM, pl.BlockSpec(memory_space=pltpu.HBM)],
        out_specs=[VM, VM, VM],
        out_shape=[shape(field), shape(strip), shape(strip)],
        scratch_shapes=[
            pltpu.VMEM(x.shape, BF16),
            pltpu.VMEM((tiles * channels * (rows + 1), 128), F32),
            pltpu.SemaphoreType.DMA((8,)),
        ],
        compiler_params=grant(8),
        cost_estimate=cost(4),
        name="prep",
    )(scal, pltpu.with_memory_space_constraint(x, pltpu.HBM))
    above, below = row_halo(head, tail)
    w_fwd, w_bwd, bias, hw, hwt, *mine = call(
        setup_kernel,
        "setup",
        [shape((channels, 9 * channels))] * 2
        + [shape((channels, 1), F32), shape((nb, channels)), shape((channels, nb))]
        + [shape((labels.shape[0] * tiles, 128))] * ncol,
        (scal, conv_weight, conv_bias[None], head_weight, labels, tail),
        us=2,
        smem=1,
    )
    together = ncol == 2 and mine[1].shape == (channels, 128)
    sides = side_columns(xt, above, below, scal, mine[1:] if together else ())
    got, xs = with_border(inner_of(xt), above, below, sides, scal)
    strips = mine[:1] + (
        got
        if together
        else [
            lax.ppermute(mine[d], "col", [(i, (i + d) % ncol) for i in range(ncol)])
            for d in range(1, ncol)
        ]
    )

    kept, got = [], []
    for stage in range(tiles):
        block = shape((pairs, rows, 128))
        hid, slope, direct, *sends = call(
            functools.partial(forward_kernel, stage=stage, swap=ncol == 2 and stage == 0),
            "forward",
            [shape(field[1:]), shape(field[1:]), shape((nb * (rows + 8), 128), F32), block, block],
            (scal, xs, w_fwd, bias, hw),
            us=6,
            smem=1,
        )
        kept.append((hid, slope, direct))
        for e in range(2):
            t = 2 * stage + e
            perm = [
                (i * ncol + j, (q * j + (i % q ^ t)) * ncol + i // q)
                for i in range(nrow)
                for j in range(ncol)
            ]
            near = [(a, b) for a, b in perm if a % ncol == b % ncol]
            far = [(a, b) for a, b in perm if a % ncol != b % ncol]
            if ncol > 2 or t == 2 * stage and t > 0:
                got.append([lax.ppermute(sends[e], ROWS, perm)])
            elif t == 0:
                first_far = far
            else:
                over = [(a, a + b % ncol - a % ncol) for a, b in far]
                along = [(a + b % ncol - a % ncol, b) for a, b in far]
                if t == 1:
                    direct_in = lax.ppermute(sends[0], ROWS, first_far + near)
                    got.append([sends[1], direct_in])
                    same = direct_in
                else:
                    same = lax.ppermute(sends[e], ROWS, near)
                relayed = lax.ppermute(sends[e], ROWS, over)
                got.append([same, lax.ppermute(relayed, ROWS, along)])

    dpre = small = ends = taps = None
    order = list(range(tiles))
    for stage in order:
        hid, slope, direct = kept[stage]
        ones, twos = got[2 * stage : 2 * stage + 2]
        args = (
            scal,
            head_bias,
            direct.reshape(nb, rows + 8, 128),
            hid,
            slope,
            hwt,
            *ones,
            *twos,
            *strips,
        )
        first, last = stage == order[0], stage == order[-1]
        dpre, small, *ends = call(
            functools.partial(
                middle_kernel, stage=stage, counts=(len(ones), len(twos)), ncol=ncol, first=first, last=last, nbins=nbins
            ),
            "middle",
            [shape(field), shape((channels, 128), F32)] + [shape(strip)] * (2 * last),
            args + (() if first else (dpre, small, taps)),
            us=5,
            smem=2,
            scratch=[
                pltpu.VMEM((nb * (rows + 8), 128), F32),
                pltpu.VMEM((channels, 128), F32),
                pltpu.VMEM((nb * 8, 128), F32),
                pltpu.VMEM((channels, 128), F32),
                pltpu.VMEM((8, 128), F32),
            ],
            aliases=None if first else {len(args): 0},
        )
        square = (wide, wide)
        pieces = shape((total // count, 128), F32)
        taps = call(
            functools.partial(weight_kernel, stage=stage, first=first),
            "weights",
            [pieces] * count if last else shape(square, F32),
            (scal, xs, dpre, small) + (() if first else (taps,)),
            us=2.5,
            mib=12,
            smem=1,
            scratch=[pltpu.VMEM(square, F32), pltpu.VMEM((total, 128), F32)] * last
            + [pltpu.VMEM((rows + 16, channels, 128), BF16)],
        )

    pieces = taps
    above, below = row_halo(*ends)
    sides = side_columns(dpre, above, below, scal)
    sides, pieces = lax.optimization_barrier((sides, pieces))
    _, ds = with_border(inner_of(dpre), above, below, sides, scal)
    parts = total_over_tiles(pieces)

    pair_gradient = pl.pallas_call(
        backward_kernel,
        grid=(rows // 16,),
        in_specs=[VM, VM],
        out_specs=pl.BlockSpec((channels, 16, width), lambda g: (0, g, 0)),
        out_shape=shape((channels, rows, width)),
        scratch_shapes=[pltpu.VMEM((tiles * channels * 24, 128), F32)],
        compiler_params=grant(8),
        cost_estimate=cost(6),
        name="backward",
    )(ds, w_bwd)

    conv_grad, biases, heads, head_biases, loss = pl.pallas_call(
        unpack_kernel,
        in_specs=[SM] + [VM] * len(parts),
        out_shape=[
            shape((3, 3, channels, channels), F32),
            shape((1, channels), F32),
            shape((nbins, channels), F32),
            shape((1, nbins), F32),
            shape((1, 1), F32),
        ],
        scratch_shapes=[pltpu.VMEM((total, 128), F32)],
        compiler_params=grant(4),
        cost_estimate=cost(1),
        name="unpack",
    )(scal, *parts)
    return (
        pair_gradient,
        conv_grad,
        biases.reshape(channels),
        heads,
        head_biases.reshape(nbins),
        loss.reshape(1),
    )


def solution(mesh):
    return jax.shard_map(
        per_device,
        mesh=mesh,
        in_specs=(
            P(None, ("parts", "row"), "col"),
            P(("parts", "row", "col"), None),
            P("parts"),
            P(),
            P(),
            P(),
            P(),
        ),
        out_specs=(
            P(None, ("parts", "row"), "col"),
            P("parts", None, None, None),
            P("parts"),
            P("parts", None),
            P("parts"),
            P("parts"),
        ),
        check_vma=False,
    )
```

```python
import functools

import jax
import jax.numpy as jnp
from jax import lax
from jax.experimental import pallas as pl
from jax.experimental.pallas import tpu as pltpu
from jax.sharding import PartitionSpec as P

DIL = 4
ROWS = ("row", "col")
F32 = jnp.float32
BF16 = jnp.bfloat16
VM = pl.BlockSpec(memory_space=pltpu.VMEM)
SM = pl.BlockSpec(memory_space=pltpu.SMEM)
MIB = 1024 * 1024


def grant(mib):
    return pltpu.CompilerParams(vmem_limit_bytes=mib * MIB)


def cost(us):
    return pl.CostEstimate(flops=int(us * 1.1e9), transcendentals=0, bytes_accessed=0)


def call(body, name, out_shape, args, us, smem=0, scratch=(), aliases=None, mib=12):
    return pl.pallas_call(
        body,
        out_shape=out_shape,
        in_specs=[SM] * smem + [VM] * (len(args) - smem),
        out_specs=jax.tree.map(lambda _: VM, out_shape),
        scratch_shapes=list(scratch),
        input_output_aliases=aliases or {},
        compiler_params=grant(mib),
        cost_estimate=cost(us),
        name=name,
    )(*args)


def shape(dims, dtype=BF16):
    return jax.ShapeDtypeStruct(dims, dtype)


def pairs_of(tiles):
    return jnp.concatenate(tiles, axis=1)


def prep_kernel(_, x, out, head, tail, landed, main, sems):
    channels, rows, width = x.shape
    tiles = width // 128
    some = channels // sems.shape[0]
    copies = [
        pltpu.make_async_copy(
            x.at[pl.ds(n * some, some)], landed.at[pl.ds(n * some, some)], sems.at[n]
        )
        for n in range(sems.shape[0])
    ]
    for copy in copies:
        copy.start()
    for n, copy in enumerate(copies):
        copy.wait()
        for c in range(n * some, (n + 1) * some):
            body = landed[c].astype(F32)
            for u in range(tiles):
                at = (u * channels + c) * (rows + 1)
                main[at : at + rows, :] = body[:, 128 * u : 128 * (u + 1)]

    def turn(i, _):
        for u in range(tiles):
            at = u * channels * (rows + 1) + i
            out[u, i] = main[pl.ds(at, channels, stride=rows + 1), :].astype(BF16)
        return 0

    lax.fori_loop(0, rows, turn, 0, unroll=8)
    for u in range(tiles):
        head[u] = out[u, :DIL]
        tail[u] = out[u, rows - DIL :]


def setup_kernel(scal, cw, cb, hw, labels, _, fwd, bwd, bias, head, headt, *pieces):
    ch = cw.shape[2]
    nbins, nb = hw.shape[0], head.shape[0]
    for a in range(3):
        for b in range(3):
            spot = (slice(ch * a, ch * (a + 1)), slice(ch * b, ch * (b + 1)))
            fwd[spot] = cw[a, b]
            bwd[spot] = cw[2 - a, 2 - b].astype(F32).T.astype(BF16)
    bias[...] = jnp.broadcast_to(cb[...], (ch, ch)).T[:, 0:1]
    full = jnp.concatenate([hw[...].astype(F32), jnp.zeros((nb - nbins, ch), F32)], axis=0)
    head[...] = full.astype(BF16)
    headt[...] = full.T.astype(BF16)
    ncol = len(pieces)
    band, width = labels.shape[0], labels.shape[1] // ncol
    blocks = [labels[:, width * n : width * (n + 1)] for n in range(ncol)]
    for d, piece in enumerate(pieces):
        want = lax.rem(scal[4] + d, ncol)
        value = blocks[0]
        for n in range(1, ncol):
            value = jnp.where(want == n, blocks[n], value)
        value = value.astype(F32).astype(BF16)
        for u in range(width // 128):
            piece[band * u : band * (u + 1), :] = value[:, 128 * u : 128 * (u + 1)]


def edges_kernel(scal, field, above, below, *sides, ncol, extra):
    tiles, rows, channels, _ = field.shape
    lane = lax.broadcasted_iota(jnp.int32, (channels, 128), 1) // DIL
    if ncol == 2:
        first = scal[4] == 0
        picks = [(jnp.where(first, tiles - 1, 0), jnp.where(first, DIL, 0))]
    else:
        picks = [(0, 0), (tiles - 1, DIL)]
    per = 128 // DIL
    if extra:
        sides[1][sides[1].shape[0] - 1] = sides[0][...]
        sides = sides[1:]
    for (tile, offset), out in zip(picks, sides):

        def add(slot, row, acc):
            turn = slot * DIL + offset
            turn = turn % 128 if isinstance(turn, int) else lax.rem(turn, 128)
            moved = pltpu.roll(row.astype(F32), turn, 1)
            return jnp.where(lane == slot, moved, acc)

        parts = out.shape[0] - extra
        for part in range(parts):
            acc = jnp.zeros((channels, 128), F32)
            start = part * per - DIL
            if part == 0:
                for ii in range(DIL):
                    acc = add(ii, above[tile, ii], acc)
                start = 0
            stop = min((part + 1) * per - DIL, rows)

            def body(i, acc):
                return add(i + DIL - part * per, field[tile, i], acc)

            for i in range(start, stop):
                acc = body(i, acc)
            if part == parts - 1:
                for ii in range(DIL):
                    acc = add(rows + DIL + ii - part * per, below[tile, ii], acc)
            out[part] = acc.astype(BF16)


def place(out, i, row):
    tiles = len(row)
    lane = lax.broadcasted_iota(jnp.int32, row[0].shape, 1)
    whole = pairs_of([v.astype(F32) for v in row])
    before = pltpu.roll(whole, DIL, 1)
    after = pltpu.roll(whole, whole.shape[1] - DIL, 1)
    for u in range(tiles):
        b = before[:, 128 * u : 128 * (u + 1)]
        a = after[:, 128 * u : 128 * (u + 1)]
        if u == 0:
            b = jnp.where(lane < DIL, 0.0, b)
        if u == tiles - 1:
            a = jnp.where(lane >= 128 - DIL, 0.0, a)
        out[u, i] = jnp.concatenate([b.astype(BF16), row[u], a.astype(BF16)], axis=0)


def inner_kernel(field, out):
    tiles, rows = field.shape[:2]

    def body(i, _):
        place(out, i + DIL, [field[u, i] for u in range(tiles)])
        return 0

    lax.fori_loop(0, rows, body, 0, unroll=64)


def border_kernel(scal, above, below, *rest, ncol):
    sides, (_, out) = rest[:-2], rest[-2:]
    tiles, high, wide, _ = out.shape
    channels = wide // 3
    for i in range(DIL):
        place(out, i, [above[u, i] for u in range(tiles)])
        place(out, i + high - DIL, [below[u, i] for u in range(tiles)])
    lane = lax.broadcasted_iota(jnp.int32, (channels, 128), 1)
    per = 128 // DIL
    if ncol == 2:
        first = scal[4] == 0
        tile = jnp.where(first, tiles - 1, 0)
        block = pl.multiple_of(jnp.where(first, 2 * channels, 0), channels)
        base = jnp.where(first, 128 - DIL, 0)
        jobs = [(sides[0], tile, block, base)]
    else:
        jobs = [(sides[0], 0, 0, 0), (sides[1], tiles - 1, 2 * channels, 128 - DIL)]
    for side, tile, block, base in jobs:
        mine = (lane >= base) & (lane < base + DIL)
        for part in range(-(-high // per)):

            def patch(ii, _):
                i = part * per + ii
                moved = pltpu.roll(
                    side[part].astype(F32), lax.rem(128 + base - ii * DIL, 128), 1
                )
                spot = (tile, i, pl.ds(block, channels))
                out[spot] = jnp.where(mine, moved, out[spot].astype(F32)).astype(BF16)
                return 0

            lax.fori_loop(0, min(per, high - part * per), patch, 0, unroll=8)


def convolved(w, row, starts, count):
    out = w.shape[0] // 3
    last = count // DIL - 1
    for m in starts:
        parts = []
        for k in range(last + 3):
            low, high = max(0, k - last), min(2, k)
            v = jnp.dot(
                w[out * low : out * (high + 1)],
                row(m + DIL * k),
                preferred_element_type=F32,
            )
            parts.append({a: v[out * (a - low) : out * (a - low + 1)] for a in range(low, high + 1)})
            if k >= 2:
                yield m + DIL * (k - 2), parts[k - 2][0] + parts[k - 1][1] + parts[k][2]


def forward_kernel(scal, xs, w, bias, hw, hid, slope, direct, one, two, *, stage, swap):
    rows, channels, _ = hid.shape
    nb = hw.shape[0]
    high = direct.shape[0] // nb
    rq = scal[0]
    u = (rq >> 1) ^ stage

    def row(i):
        return pairs_of([xs[u, i], xs[u, i + 1]])

    for i, pre in convolved(w, row, range(0, DIL, 2), rows):
        pre = pre + bias[...]
        grown = jnp.exp(jnp.minimum(pre, 0.0))
        h = jnp.where(pre > 0, pre, grown - 1.0).astype(BF16)
        s = jnp.where(pre > 0, 1.0, grown).astype(BF16)
        for e in range(2):
            hid[i + e] = h[:, 128 * e : 128 * (e + 1)]
            slope[i + e] = s[:, 128 * e : 128 * (e + 1)]

    def head(g, _):
        for p in range(8):
            i = g * 64 + 8 * p
            d = jnp.dot(hw[...], pairs_of([hid[i + e] for e in range(8)]), preferred_element_type=F32)
            for e in range(8):
                direct[pl.ds(i + e, nb, stride=high), :] = d[:, 128 * e : 128 * (e + 1)]
        return 0

    lax.fori_loop(0, rows // 64, head, 0)

    flip = ((rq & 1) ^ (1 - scal[5] if swap else 0)) == 1
    for m in range(one.shape[0]):
        both = [direct[high * k : high * k + rows, :] for k in (2 * m, 2 * m + 1)]
        turned = jnp.concatenate(both, axis=0).T.astype(BF16)
        upper, lower = turned[:rows].astype(F32), turned[rows:].astype(F32)
        one[m] = jnp.where(flip, lower, upper).astype(BF16)
        two[m] = jnp.where(flip, upper, lower).astype(BF16)


def middle_kernel(scal, hb, direct, hid, slope, hwt, *rest, stage, counts, ncol, first, last, nbins):
    ones, twos, rest = rest[: counts[0]], rest[counts[0] : sum(counts)], rest[sum(counts) :]
    strips, rest = rest[:ncol], rest[ncol:]
    if not first:
        before, rest = rest[1], rest[3:]
    dpre, small, *ends, dl, hacc, bacc, cacc, lacc = rest
    nb, high, _ = direct.shape
    rows = hid.shape[0]
    band = rows // ncol
    channels = hwt.shape[0]
    rq, extent = scal[0], scal[3]
    u = (rq >> 1) ^ stage
    flip = (rq & 1) == 1
    crossed = scal[5] == 1
    for ref in (hacc, bacc, cacc, lacc):
        ref[...] = jnp.zeros_like(ref)
    dl[nbins * high :, :] = jnp.zeros((dl.shape[0] - nbins * high, 128), F32)

    lane = lax.broadcasted_iota(jnp.int32, (8, 128), 1)
    low = lane < 64
    col_ids = scal[2] + 128 * u + lane
    area = (extent * extent).astype(F32)

    def softmax(g, _):
        base = pl.multiple_of(g * 8, 8)
        row_ids = scal[1] + base + lax.broadcasted_iota(jnp.int32, (8, 128), 0)
        valid = jnp.where((row_ids < extent) & (col_ids < extent), 1.0, 0.0)
        strip, at = base // band, pl.multiple_of(lax.rem(base, band), 8)
        wanted = jnp.zeros((8, 128), F32)
        for d in range(ncol):
            here = lax.rem(scal[4] + ncol - strip, ncol) == d
            rows8 = pl.ds(pl.multiple_of(u * band + at, 8), 8)
            if len(strips[d].shape) == 3:
                value = strips[d][strips[d].shape[0] - 1, rows8, :]
            else:
                value = strips[d][rows8, :]
            wanted = jnp.where(here, value.astype(F32), wanted)
        logits = []
        for m in range((nbins + 1) // 2):
            a, b = (
                [ref[m, pl.ds(base, 8), :].astype(F32) for ref in refs] for refs in (ones, twos)
            )
            a = a[0] if len(a) == 1 else jnp.where(crossed, a[1], a[0])
            b = b[0] if len(b) == 1 else jnp.where(crossed, b[1], b[0])
            a, b = jnp.where(flip, b, a), jnp.where(flip, a, b)
            mirror = (
                jnp.where(low, a, pltpu.roll(b, 64, 1)),
                jnp.where(low, pltpu.roll(a, 64, 1), b),
            )
            for k in range(2 * m, min(2 * m + 2, nbins)):
                logits.append(
                    0.5 * (direct[k, pl.ds(base, 8), :] + mirror[k - 2 * m]) + hb[k]
                )
        peak = functools.reduce(jnp.maximum, logits)
        picked = functools.reduce(
            lambda a, b: a + b,
            [jnp.where(wanted == k, logits[k], 0.0) for k in range(nbins)],
        )
        powers = [jnp.exp(v - peak) for v in logits]
        total = functools.reduce(lambda a, b: a + b, powers)
        lacc[...] += valid * (peak + jnp.log(total) - picked)
        inverse = 1.0 / total
        scale = valid / area
        for k in range(nbins):
            d = (powers[k] * inverse - jnp.where(wanted == k, 1.0, 0.0)) * scale
            d = d.astype(BF16).astype(F32)
            dl[pl.ds(k * high + base, 8), :] = d
            bacc[8 * k : 8 * k + 8, :] += d
        return 0

    lax.fori_loop(0, rows // 8, softmax, 0, unroll=2)

    def back(g, _):
        heads, shifts = [], []
        for p in range(8):
            i = g * 64 + 8 * p
            d = pairs_of(
                [dl[pl.ds(i + e, nb, stride=high), :].astype(BF16) for e in range(8)]
            )
            h = pairs_of([hid[i + e] for e in range(8)])
            s = pairs_of([slope[i + e] for e in range(8)])
            v = jnp.dot(hwt[...], d, preferred_element_type=F32) * s.astype(F32)
            v = v.astype(BF16)
            for e in range(8):
                dpre[u, i + e] = v[:, 128 * e : 128 * (e + 1)]
                shifts.append(v[:, 128 * e : 128 * (e + 1)].astype(F32))
            heads.append((d, h))
        cacc[...] += functools.reduce(lambda a, b: a + b, shifts)
        hacc[0:nb, 0:channels] += lax.dot_general(
            pairs_of([d for d, _ in heads]), pairs_of([h for _, h in heads]),
            (((1,), (1,)), ((), ())), preferred_element_type=F32,
        )
        return 0

    lax.fori_loop(0, rows // 64, back, 0)

    spot = lax.broadcasted_iota(jnp.int32, small.shape, 1)
    sums = jnp.sum(bacc[...].reshape(nb, 8, 128), axis=1)
    sums = jnp.sum(sums, axis=1, keepdims=True)
    sums = jnp.concatenate([sums, jnp.zeros((channels - nb, 1), F32)], axis=0)
    biases = jnp.sum(cacc[...], axis=1, keepdims=True)
    loss = jnp.sum(jnp.sum(lacc[...], axis=1, keepdims=True), axis=0, keepdims=True)
    value = jnp.where(
        spot < channels,
        hacc[...],
        jnp.where(spot == channels, sums, jnp.where(spot == channels + 1, biases, loss)),
    )
    small[...] = value if first else value + before[...]
    if last:
        for v in range(dpre.shape[0]):
            ends[0][v] = dpre[v, :DIL]
            ends[1][v] = dpre[v, rows - DIL :]


def sum_kernel(*refs):
    refs[-1][...] = functools.reduce(lambda a, b: a + b, [ref[...] for ref in refs[:-1]])


def sum_of(values):
    return call(sum_kernel, "sum", shape(values[0].shape, F32), tuple(values), us=0.5, mib=2)


def weight_kernel(scal, xs, dpre, small, *rest, stage, first):
    if not first:
        before, rest = rest[0], rest[1:]
    padded, outs = rest[-1], rest[:-1]
    _, rows, channels, _ = dpre.shape
    wide = 3 * channels
    u = (scal[0] >> 1) ^ stage
    padded[0:8] = jnp.zeros((8, channels, 128), BF16)
    padded[8 : 8 + rows] = dpre[u]
    padded[8 + rows :] = jnp.zeros((8, channels, 128), BF16)

    def body(g, acc):
        left, right = [], []
        for ii in range(3 * 24):
            i = g * 72 + ii
            left.append(
                jnp.concatenate([padded[i + 8 - DIL * a] for a in range(3)], axis=0)
            )
            right.append(xs[u, i])
        acc[...] += lax.dot_general(
            pairs_of(left), pairs_of(right), (((1,), (1,)), ((), ())),
            preferred_element_type=F32,
        )

    acc = outs[-1] if len(outs) == 1 else outs[-2]
    acc[...] = jnp.zeros_like(acc) if first else before[...]
    lax.fori_loop(0, (rows + 8) // 72, lambda g, _: body(g, acc), None)
    if len(outs) == 1:
        return
    out, outs = outs[-1], outs[:-2]
    half = wide // 2
    out[0:wide, :] = acc[:, 0:128]
    out[wide : wide + half, 0:64] = acc[0:half, 128:192]
    out[wide : wide + half, 64:128] = acc[half:wide, 128:192]
    out[wide + half :, :] = small[...]
    for n, piece in enumerate(outs):
        size = piece.shape[0]
        piece[...] = out[pl.ds(pl.multiple_of((scal[6] ^ n) * size, 8), size), :]


def backward_kernel(ds, w, out, turned):
    step = pl.program_id(0)
    channels, some, width = out.shape
    tiles = width // 128
    def row(i):
        return pairs_of([ds[u, step * some + i] for u in range(tiles)])

    for i, v in convolved(w, row, range(DIL), some):
        for u in range(tiles):
            at = u * channels * (some + 8) + i
            turned[pl.ds(at, channels, stride=some + 8), :] = v[:, 128 * u : 128 * (u + 1)]
    for u in range(tiles):
        at = (some + 8) * channels * u
        block = turned[at : at + (some + 8) * channels, :].reshape(channels, some + 8, 128)
        out[:, :, 128 * u : 128 * (u + 1)] = block[:, :some].astype(BF16)


def side_columns(field, above, below, scal, more=()):
    parts = -(-(field.shape[1] + 2 * DIL) * DIL // 128)
    ncol = lax.axis_size("col")
    return call(
        functools.partial(edges_kernel, ncol=ncol, extra=len(more)),
        "edges",
        [shape((parts + len(more), field.shape[2], 128))] * (1 if ncol == 2 else 2),
        (scal, field, above, below, *more),
        us=1.5,
        smem=1,
    )


def with_border(inner, above, below, sides, scal):
    ncol = lax.axis_size("col")
    if ncol == 2:
        got = [lax.ppermute(sides[0], "col", [(0, 1), (1, 0)])]
    else:
        to_left, to_right = sides
        got = [
            lax.ppermute(to_right, "col", [(i, i + 1) for i in range(ncol - 1)]),
            lax.ppermute(to_left, "col", [(i + 1, i) for i in range(ncol - 1)]),
        ]
    return got, call(
        functools.partial(border_kernel, ncol=ncol),
        "border",
        shape(inner.shape),
        (scal, above, below, *got, inner),
        us=1.5,
        smem=1,
        aliases={3 + len(got): 0},
    )


def inner_of(field):
    tiles, rows, channels, _ = field.shape
    return call(
        inner_kernel,
        "inner",
        shape((tiles, rows + 2 * DIL, 3 * channels, 128)),
        (field,),
        us=3,
    )


def row_halo(head, tail):
    count = lax.axis_size("row")
    above = lax.ppermute(tail, "row", [(i, i + 1) for i in range(count - 1)])
    below = lax.ppermute(head, "row", [(i + 1, i) for i in range(count - 1)])
    return above, below


def piece_count(total):
    nrow, ncol = lax.axis_size("row"), lax.axis_size("col")
    return 4 if ncol == 2 and nrow % 2 == 0 and nrow <= 8 and total % 32 == 0 else 1


def total_over_tiles(pieces):
    nrow, ncol = lax.axis_size("row"), lax.axis_size("col")
    if len(pieces) == 4:
        def near(v, d):
            perm = [
                (i * 2 + j, (i ^ (d >> 1)) * 2 + (j ^ (d & 1)))
                for i in range(nrow)
                for j in range(2)
            ]
            return lax.ppermute(v, ROWS, perm)

        own = sum_of([pieces[0]] + [near(pieces[d], d) for d in (1, 2, 3)])
        turns = [[(i, (i + 2 * d) % nrow) for i in range(nrow)] for d in range(1, nrow // 2)]
        own = sum_of([own] + [lax.ppermute(own, "row", turn) for turn in turns])
        return [own] + [near(own, d) for d in (1, 2, 3)]
    value = pieces[0]
    for axis, count in (("col", ncol), ("row", nrow)):
        if count & (count - 1):
            value = lax.psum(value, axis)
            continue
        bit = 1
        while bit < count:
            value = value + lax.ppermute(value, axis, [(i, i ^ bit) for i in range(count)])
            bit *= 2
    return [value]


def unpack_kernel(scal, *rest):
    parts, (taps, biases, heads, head_biases, loss, buf) = rest[:-6], rest[-6:]
    for n, part in enumerate(parts):
        size = part.shape[0]
        buf[pl.ds(pl.multiple_of((scal[6] ^ n) * size, 8), size), :] = part[...]
    ch = taps.shape[2]
    half = 3 * ch // 2
    for a in range(3):
        taps[a, 0] = buf[a * ch : (a + 1) * ch, 0:ch]
        taps[a, 1] = buf[a * ch : (a + 1) * ch, ch : 2 * ch]
        for o in range(0, ch, 32):
            at = a * ch + o
            lanes = slice(0, ch) if at < half else slice(ch, 2 * ch)
            row = 3 * ch + at % half
            taps[a, 2, o : o + 32] = buf[row : row + 32, lanes]
    small = buf[3 * ch + half :, :]
    turned = small.T
    heads[...] = small[: heads.shape[0], :ch]
    head_biases[...] = turned[ch : ch + 1, : heads.shape[0]]
    biases[...] = turned[ch + 1 : ch + 2, :]
    area = (scal[3] * scal[3]).astype(F32)
    loss[...] = turned[ch + 2 : ch + 3, 0:1] / area


def per_device(x, labels, lengths, conv_weight, conv_bias, head_weight, head_bias):
    channels, rows, width = x.shape
    nbins = head_weight.shape[0]
    nrow, ncol = lax.axis_size("row"), lax.axis_size("col")
    q = width // rows
    tiles = width // 128
    assert rows == 64 and channels == 64 and q == 2 * tiles and q & (q - 1) == 0
    assert q * ncol == nrow and 128 * tiles == width
    nb = -(-nbins // 8) * 8
    pairs = (nbins + 1) // 2
    wide = 3 * channels
    total = wide + wide // 2 + channels
    r, c = lax.axis_index("row"), lax.axis_index("col")

    count = piece_count(total)
    mine = (r % 2) * 2 + c if count == 4 else 0 * r
    crossed = (r // q != c).astype(jnp.int32)
    scal = jnp.stack([r % q, r * rows, c * width, lengths[0], c, crossed, mine]).astype(jnp.int32)
    field = (tiles, rows, channels, 128)
    strip = (tiles, DIL, channels, 128)
    xt, head, tail = pl.pallas_call(
        prep_kernel,
        in_specs=[SM, pl.BlockSpec(memory_space=pltpu.HBM)],
        out_specs=[VM, VM, VM],
        out_shape=[shape(field), shape(strip), shape(strip)],
        scratch_shapes=[
            pltpu.VMEM(x.shape, BF16),
            pltpu.VMEM((tiles * channels * (rows + 1), 128), F32),
            pltpu.SemaphoreType.DMA((8,)),
        ],
        compiler_params=grant(8),
        cost_estimate=cost(4),
        name="prep",
    )(scal, pltpu.with_memory_space_constraint(x, pltpu.HBM))
    above, below = row_halo(head, tail)
    w_fwd, w_bwd, bias, hw, hwt, *mine = call(
        setup_kernel,
        "setup",
        [shape((wide, wide))] * 2
        + [shape((channels, 1), F32), shape((nb, channels)), shape((channels, nb))]
        + [shape((labels.shape[0] * tiles, 128))] * ncol,
        (scal, conv_weight, conv_bias[None], head_weight, labels, tail),
        us=2,
        smem=1,
    )
    together = ncol == 2 and mine[1].shape == (channels, 128)
    sides = side_columns(xt, above, below, scal, mine[1:] if together else ())
    got, xs = with_border(inner_of(xt), above, below, sides, scal)
    strips = mine[:1] + (
        got
        if together
        else [
            lax.ppermute(mine[d], "col", [(i, (i + d) % ncol) for i in range(ncol)])
            for d in range(1, ncol)
        ]
    )

    kept, got = [], []
    for stage in range(tiles):
        block = shape((pairs, rows, 128))
        hid, slope, direct, *sends = call(
            functools.partial(forward_kernel, stage=stage, swap=ncol == 2 and stage == 0),
            "forward",
            [shape(field[1:]), shape(field[1:]), shape((nb * (rows + 8), 128), F32), block, block],
            (scal, xs, w_fwd, bias, hw),
            us=6,
            smem=1,
        )
        kept.append((hid, slope, direct))
        for e in range(2):
            t = 2 * stage + e
            perm = [
                (i * ncol + j, (q * j + (i % q ^ t)) * ncol + i // q)
                for i in range(nrow)
                for j in range(ncol)
            ]
            near = [(a, b) for a, b in perm if a % ncol == b % ncol]
            far = [(a, b) for a, b in perm if a % ncol != b % ncol]
            if ncol > 2 or t == 2 * stage and t > 0:
                got.append([lax.ppermute(sends[e], ROWS, perm)])
            elif t == 0:
                first_far = far
            else:
                over = [(a, a + b % ncol - a % ncol) for a, b in far]
                along = [(a + b % ncol - a % ncol, b) for a, b in far]
                if t == 1:
                    direct_in = lax.ppermute(sends[0], ROWS, first_far + near)
                    got.append([sends[1], direct_in])
                    same = direct_in
                else:
                    same = lax.ppermute(sends[e], ROWS, near)
                relayed = lax.ppermute(sends[e], ROWS, over)
                got.append([same, lax.ppermute(relayed, ROWS, along)])

    dpre = small = ends = taps = None
    order = list(range(tiles))
    for stage in order:
        hid, slope, direct = kept[stage]
        ones, twos = got[2 * stage : 2 * stage + 2]
        args = (
            scal,
            head_bias,
            direct.reshape(nb, rows + 8, 128),
            hid,
            slope,
            hwt,
            *ones,
            *twos,
            *strips,
        )
        first, last = stage == order[0], stage == order[-1]
        dpre, small, *ends = call(
            functools.partial(
                middle_kernel, stage=stage, counts=(len(ones), len(twos)), ncol=ncol, first=first, last=last, nbins=nbins
            ),
            "middle",
            [shape(field), shape((channels, 128), F32)] + [shape(strip)] * (2 * last),
            args + (() if first else (dpre, small, taps)),
            us=5,
            smem=2,
            scratch=[
                pltpu.VMEM((nb * (rows + 8), 128), F32),
                pltpu.VMEM((channels, 128), F32),
                pltpu.VMEM((nb * 8, 128), F32),
                pltpu.VMEM((channels, 128), F32),
                pltpu.VMEM((8, 128), F32),
            ],
            aliases=None if first else {len(args): 0},
        )
        square = (wide, wide)
        pieces = shape((total // count, 128), F32)
        taps = call(
            functools.partial(weight_kernel, stage=stage, first=first),
            "weights",
            [pieces] * count if last else shape(square, F32),
            (scal, xs, dpre, small) + (() if first else (taps,)),
            us=2.5,
            mib=12,
            smem=1,
            scratch=[pltpu.VMEM(square, F32), pltpu.VMEM((total, 128), F32)] * last
            + [pltpu.VMEM((rows + 16, channels, 128), BF16)],
        )

    pieces = taps
    above, below = row_halo(*ends)
    sides = side_columns(dpre, above, below, scal)
    sides, pieces = lax.optimization_barrier((sides, pieces))
    _, ds = with_border(inner_of(dpre), above, below, sides, scal)
    parts = total_over_tiles(pieces)

    pair_gradient = pl.pallas_call(
        backward_kernel,
        grid=(rows // 16,),
        in_specs=[VM, VM],
        out_specs=pl.BlockSpec((channels, 16, width), lambda g: (0, g, 0)),
        out_shape=shape((channels, rows, width)),
        scratch_shapes=[pltpu.VMEM((tiles * channels * 24, 128), F32)],
        compiler_params=grant(8),
        cost_estimate=cost(6),
        name="backward",
    )(ds, w_bwd)

    conv_grad, biases, heads, head_biases, loss = pl.pallas_call(
        unpack_kernel,
        in_specs=[SM] + [VM] * len(parts),
        out_shape=[
            shape((3, 3, channels, channels), F32),
            shape((1, channels), F32),
            shape((nbins, channels), F32),
            shape((1, nbins), F32),
            shape((1, 1), F32),
        ],
        scratch_shapes=[pltpu.VMEM((total, 128), F32)],
        compiler_params=grant(4),
        cost_estimate=cost(1),
        name="unpack",
    )(scal, *parts)
    return (
        pair_gradient,
        conv_grad,
        biases.reshape(channels),
        heads,
        head_biases.reshape(nbins),
        loss.reshape(1),
    )


def solution(mesh):
    return jax.shard_map(
        per_device,
        mesh=mesh,
        in_specs=(
            P(None, ("parts", "row"), "col"),
            P(("parts", "row", "col"), None),
            P("parts"),
            P(),
            P(),
            P(),
            P(),
        ),
        out_specs=(
            P(None, ("parts", "row"), "col"),
            P("parts", None, None, None),
            P("parts"),
            P("parts", None),
            P("parts"),
            P("parts"),
        ),
        check_vma=False,
    )
```
